512 devices in a mesh: dp: 2 (over core), ctx: 64 (over z, x), tp: 4 (over y).
Axes of the slice: x: 4, y: 4, z: 16, core: 2. Of those that a mesh axis runs over, the one named last changes fastest.
Arguments:
- query: bfloat16 [2, 8192, 8192], P('dp', 'ctx', 'tp'), may hold values from -80 to 80
- key: bfloat16 [2, 8192, 1024], P('dp', 'ctx', 'tp'), may hold values from -6 to 6
- value: bfloat16 [2, 8192, 1024], P('dp', 'ctx', 'tp'), may hold values from -6 to 6
- key_shift: float32 [2, 8192, 1024], P('dp', 'ctx', 'tp'), may hold values from -0.6 to 0.6
- value_shift: float32 [2, 8192, 1024], P('dp', 'ctx', 'tp'), may hold values from -0.6 to 0.6
- doc_ids: int32 [2, 8192], P('dp', 'ctx'), may hold values from 0 to 31, never falling along the last dimension, each value on 1 to 2048 neighbouring positions
- target: bfloat16 [2, 8192, 8192], P('dp', 'ctx', 'tp'), may hold values from -160 to 160
Outputs:
- attn: bfloat16 [2, 8192, 8192], P('dp', 'ctx', 'tp')
- new_key_shift: float32 [2, 8192, 1024], P('dp', 'ctx', 'tp')
- new_value_shift: float32 [2, 8192, 1024], P('dp', 'ctx', 'tp')
The draws below stay inside these ranges and needn't reach their ends.
All inputs are finite; a program needn't handle non-finite values.
Results may differ from the reference program's by a relative error of at most 0.005.
Values may be sent and summed in bfloat16 or wider, within the bound.
No kernel may reach another device: no remote copies, remote signals or barrier semaphores. Data moves between devices by JAX's collectives and lax.ppermute only.
A program may use at most 128 MiB of HBM per device.

```python
import math
import jax
import jax.numpy as jnp
import numpy as np
from jax import lax

HEADS = 64
KV_HEADS = 8
HEAD = 128
BATCH = 2
SEQ = 8192
DOC_MAX = 2048
DOCS = 32


def shared_keys(key):
    shape = (BATCH, SEQ, KV_HEADS, HEAD)
    base = jax.random.truncated_normal(jax.random.fold_in(key, 11), -6.0, 6.0, shape, jnp.float32)
    return base


def draw_key(key, part):
    return shared_keys(key).reshape(BATCH, SEQ, KV_HEADS * HEAD).astype(jnp.bfloat16)


def draw_query(key, part):
    groups = HEADS // KV_HEADS
    shape = (BATCH, SEQ, KV_HEADS, groups, HEAD)
    drawn = jax.random.truncated_normal(jax.random.fold_in(key, 21), -6.0, 6.0, shape, jnp.float32)
    return drawn.reshape(BATCH, SEQ, HEADS * HEAD).astype(jnp.bfloat16)


def draw_target(key, part):
    shape = (BATCH, SEQ, HEADS * HEAD)
    ramp = jnp.exp(jnp.log(3.0) * jnp.arange(SEQ, dtype=jnp.float32) / SEQ)[None, :, None]
    drawn = jax.random.truncated_normal(jax.random.fold_in(key, 31), -5.0, 5.0, shape, jnp.float32)
    return (drawn * ramp).astype(jnp.bfloat16)


def block_levels(own_key, dims, pieces, smallest, top_value):
    gain, own = 1.0, jax.random.fold_in(own_key, 6)
    for position, shards_of in pieces:
        heights = jnp.exp(jax.random.uniform(jax.random.fold_in(own, position), (shards_of,), jnp.float32, smallest / len(pieces), top_value / len(pieces)))
        gain = gain * jnp.repeat(heights, dims[position] // shards_of).reshape([-1 if axis == position else 1 for axis in range(len(dims))])
    return gain


def split_up(count, total, most, lean):
    weights = [(1 << 20) // math.isqrt(rank ** lean) + 1 for rank in range(2, count + 1)]
    rest, counts = total - most - (count - 1), [1] * (count - 1)
    while rest > 0:
        movable = [i for i in range(count - 1) if counts[i] < most]
        whole, budget = sum([weights[i] for i in movable]), rest
        for i in movable:
            addition = min(most - counts[i], max(1, budget * weights[i] // whole), rest)
            counts[i] = counts[i] + addition
            rest = rest - addition
    return np.array([most] + counts)


def uneven(rng, number_of, total, limit, lean):
    if number_of == 2:
        one = jax.random.randint(rng, (), max(1, total - limit), min(limit, total - 1) + 1)
        return jnp.stack([one, total - one])
    tallies = jnp.asarray(split_up(number_of, total, limit, lean), jnp.int32)
    couples = (number_of - 1) // 2
    source_of, taker = tallies[1:1 + 2 * couples:2], tallies[2:2 + 2 * couples:2]
    slack = jnp.minimum(source_of - 1, limit - taker)
    shifted = jax.random.randint(jax.random.fold_in(rng, 1), (couples,), 0, 1 << 20) % (slack + 1)
    tallies = tallies.at[1:1 + 2 * couples:2].set(source_of - shifted).at[2:2 + 2 * couples:2].set(taker + shifted)
    return tallies[jax.random.permutation(jax.random.fold_in(rng, 2), number_of)]


def bell_draw(own_key, dims, spread, limit, shards=(), held_as=jnp.bfloat16):
    gain = block_levels(own_key, dims, shards, -0.22, 0.18) if shards else 1.0
    entries = jax.random.normal(own_key, dims, jnp.float32) * spread * gain
    return jnp.minimum(jnp.maximum(entries, -limit), limit).astype(held_as)


def setup_inputs(seed: int = 0) -> dict:
    seeds = jax.random.split(jax.random.key(seed), 8)
    return {
        "query": draw_query(jax.random.fold_in(seeds[7], 71), 0),
        "key": draw_key(jax.random.fold_in(seeds[7], 71), 0),
        "value": bell_draw(seeds[2], (BATCH, SEQ, KV_HEADS * HEAD), 1.0, 6.0, ((0, 2), (1, 64), (2, 4))),
        "key_shift": bell_draw(seeds[3], (BATCH, SEQ, KV_HEADS * HEAD), 0.1, 0.6, ((0, 2), (1, 64), (2, 4)), jnp.float32),
        "value_shift": bell_draw(seeds[4], (BATCH, SEQ, KV_HEADS * HEAD), 0.1, 0.6, ((0, 2), (1, 64), (2, 4)), jnp.float32),
        "doc_ids": jax.vmap(lambda own: jnp.searchsorted(jnp.cumsum(uneven(own, DOCS, SEQ, DOC_MAX, 2)), jnp.arange(SEQ), side="right"))(jax.random.split(seeds[5], BATCH)).reshape((BATCH, SEQ)).astype(jnp.int32),
        "target": draw_target(jax.random.fold_in(seeds[7], 71), 0),
    }


step_size = 0.1
radius_scale = 0.13

def reference(query, key, value, key_shift, value_shift, doc_ids, target):
    group = HEADS // KV_HEADS
    block = min(512, SEQ)
    width = DOC_MAX + block
    scale = 1.0 / math.sqrt(HEAD)
    key_new = (key.astype(jnp.float32) + key_shift).astype(jnp.bfloat16)
    val_new = (value.astype(jnp.float32) + value_shift).astype(jnp.bfloat16)
    outs = []
    grad_keys = []
    grad_vals = []
    for batch_row in range(BATCH):
        q_all = query[batch_row].reshape(SEQ, KV_HEADS, group, HEAD)
        t_all = target[batch_row].reshape(SEQ, KV_HEADS, group, HEAD)
        k_pad = jnp.concatenate([jnp.zeros((DOC_MAX, KV_HEADS, HEAD), key_new.dtype), key_new[batch_row].reshape(SEQ, KV_HEADS, HEAD)], 0)
        v_pad = jnp.concatenate([jnp.zeros((DOC_MAX, KV_HEADS, HEAD), val_new.dtype), val_new[batch_row].reshape(SEQ, KV_HEADS, HEAD)], 0)
        d_pad = jnp.concatenate([-jnp.ones((DOC_MAX,), jnp.int32), doc_ids[batch_row].astype(jnp.int32)], 0)
        own_docs = doc_ids[batch_row].astype(jnp.int32)

        def one_block(carry, start):
            grad_k, grad_v = carry
            q_blk = lax.dynamic_slice_in_dim(q_all, start, block, 0)
            t_blk = lax.dynamic_slice_in_dim(t_all, start, block, 0)
            k_win = lax.dynamic_slice_in_dim(k_pad, start, width, 0)
            v_win = lax.dynamic_slice_in_dim(v_pad, start, width, 0)
            d_win = lax.dynamic_slice_in_dim(d_pad, start, width, 0)
            d_blk = lax.dynamic_slice_in_dim(own_docs, start, block, 0)
            q_pos = start + jnp.arange(block, dtype=jnp.int32)
            k_pos = start - DOC_MAX + jnp.arange(width, dtype=jnp.int32)
            allowed = (d_win[None, :] == d_blk[:, None]) & (k_pos[None, :] <= q_pos[:, None]) & (k_pos[None, :] >= 0)

            def per_head(items):
                q_head, t_head, k_head, v_head = items
                qf = q_head.astype(jnp.float32)
                tf = t_head.astype(jnp.float32)
                kf = k_head.astype(jnp.float32)
                vf = v_head.astype(jnp.float32)
                scores = jnp.einsum('tgd,wd->gtw', qf, kf) * scale
                scores = jnp.where(allowed[None], scores, -jnp.inf)
                top = lax.optimization_barrier(jnp.max(scores, -1, keepdims=True))
                expo = jnp.exp(scores - top)
                total = lax.optimization_barrier(jnp.sum(expo, -1, keepdims=True))
                expo16 = expo.astype(jnp.bfloat16)
                out = jnp.einsum('gtw,wd->gtd', expo16.astype(jnp.float32), vf) / total
                dprob = jnp.einsum('tgd,wd->gtw', tf, vf)
                delta = lax.optimization_barrier(jnp.sum(jnp.transpose(tf, (1, 0, 2)) * out, -1, keepdims=True))
                prob = expo / total
                ds16 = (prob * (dprob - delta)).astype(jnp.bfloat16)
                prob16 = prob.astype(jnp.bfloat16)
                dk = jnp.einsum('gtw,tgd->wd', ds16.astype(jnp.float32), qf) * scale
                dv = jnp.einsum('gtw,tgd->wd', prob16.astype(jnp.float32), tf)
                return (jnp.transpose(out.astype(jnp.bfloat16), (1, 0, 2)), dk, dv)
            out_blk, dk_blk, dv_blk = lax.map(per_head, (jnp.transpose(q_blk, (1, 0, 2, 3)), jnp.transpose(t_blk, (1, 0, 2, 3)), jnp.transpose(k_win, (1, 0, 2)), jnp.transpose(v_win, (1, 0, 2))))
            old_k = lax.dynamic_slice_in_dim(grad_k, start, width, 0)
            old_v = lax.dynamic_slice_in_dim(grad_v, start, width, 0)
            grad_k = lax.dynamic_update_slice_in_dim(grad_k, old_k + jnp.transpose(dk_blk, (1, 0, 2)), start, 0)
            grad_v = lax.dynamic_update_slice_in_dim(grad_v, old_v + jnp.transpose(dv_blk, (1, 0, 2)), start, 0)
            return ((grad_k, grad_v), jnp.transpose(out_blk, (1, 0, 2, 3)).reshape(block, HEADS * HEAD))
        starts = (jnp.arange(SEQ // block, dtype=jnp.int32) * block).astype(jnp.int32)
        zero_grad = jnp.zeros((DOC_MAX + SEQ, KV_HEADS, HEAD), jnp.float32)
        (grad_k, grad_v), out_blocks = lax.scan(one_block, (zero_grad, zero_grad), starts)
        outs.append(out_blocks.reshape(SEQ, HEADS * HEAD))
        grad_keys.append(grad_k[DOC_MAX:].reshape(SEQ, KV_HEADS * HEAD))
        grad_vals.append(grad_v[DOC_MAX:].reshape(SEQ, KV_HEADS * HEAD))
    attn = jnp.stack(outs, 0)
    grad_key = jnp.stack(grad_keys, 0)
    grad_val = jnp.stack(grad_vals, 0)
    count = BATCH * SEQ * 2 * KV_HEADS * HEAD
    rms = jnp.sqrt((jnp.sum(grad_key * grad_key) + jnp.sum(grad_val * grad_val)) / count + 1e-05)
    moved_key = key_shift + step_size / rms * grad_key
    moved_val = value_shift + step_size / rms * grad_val
    size_sq = lax.optimization_barrier(jnp.sum(moved_key * moved_key, -1, keepdims=True)) + lax.optimization_barrier(jnp.sum(moved_val * moved_val, -1, keepdims=True))
    radius = radius_scale * math.sqrt(2 * KV_HEADS * HEAD)
    factor = jnp.minimum(1.0, radius / jnp.sqrt(size_sq + 1e-06))
    return (attn, moved_key * factor, moved_val * factor)
```

```python
import functools
import math

import jax
import jax.numpy as jnp
from jax import lax
from jax.experimental import pallas as pl
from jax.experimental.pallas import tpu as pltpu
from jax.sharding import Mesh
from jax.sharding import PartitionSpec as P

HEADS = 64
KV_HEADS = 8
HEAD = 128
GROUP = HEADS // KV_HEADS
DOC_MAX = 2048

step_size = 0.1
radius_scale = 0.13

BF = jnp.bfloat16
F32 = jnp.float32
NT = (((1,), (1,)), ((), ()))
NN = (((1,), (0,)), ((), ()))
FAR = -1e30


def mm(a, b, dims=NN):
    return lax.dot_general(a, b, dims, preferred_element_type=F32)


def attn_kernel(
    own_rows, side_rows, q_ref, t_ref, own_ref, r1_ref, r2_ref, r3_ref, docs_ref,
    o_ref, gown_ref, g1_ref, g2_ref, g3_ref,
    kaug, vaug, vat, qaug, taug, s_ref, p_ref,
):
    tokens = q_ref.shape[0]
    rows_all = GROUP * tokens
    blocks = [(own_ref, gown_ref, b) for b in range(own_rows)]
    for r, g in ((r1_ref, g1_ref), (r2_ref, g2_ref), (r3_ref, g3_ref)):
        blocks += [(r, g, b) for b in range(side_rows)]
    docs = docs_ref[...]
    docs_sq = jnp.concatenate([docs, jnp.zeros((tokens - docs.shape[0], tokens), F32)], 0)
    doc_cols = docs_sq.T
    doc_row = docs[own_rows - 1 : own_rows, :]
    i_key = lax.broadcasted_iota(jnp.int32, (tokens, tokens), 0)
    i_qry = lax.broadcasted_iota(jnp.int32, (tokens, tokens), 1)
    one = jnp.ones((tokens, HEAD), BF)
    for j, (src, _, b) in enumerate(blocks):
        rows = slice(j * tokens, (j + 1) * tokens)
        kaug[rows, 0:HEAD] = src[b * tokens : (b + 1) * tokens, 0:HEAD]
        v = src[b * tokens : (b + 1) * tokens, HEAD : 2 * HEAD]
        vaug[rows, 0:HEAD] = v
        vaug[rows, HEAD : 2 * HEAD] = one
        vat[0:HEAD, rows] = v.T
        vat[HEAD : 2 * HEAD, rows] = one
        ok = doc_cols[:, j : j + 1] == doc_row
        if j == own_rows - 1:
            ok = ok & (i_key <= i_qry)
        kaug[rows, HEAD : HEAD + tokens] = jnp.where(ok, 0.0, FAR).astype(BF)
    eye = (i_key == i_qry).astype(F32).astype(BF)
    for h in range(GROUP):
        qaug[h * tokens : (h + 1) * tokens, 0:HEAD] = q_ref[:, h * HEAD : (h + 1) * HEAD]
        qaug[h * tokens : (h + 1) * tokens, HEAD : HEAD + tokens] = eye
    top = jnp.full((8, rows_all), -3e38, F32)
    for j in range(len(blocks)):
        rows = slice(j * tokens, (j + 1) * tokens)
        s = mm(kaug[rows, :], qaug[...], NT)
        s_ref[rows, :] = s
        top = jnp.maximum(top, jnp.max(s.reshape(tokens // 8, 8, rows_all), 0))
    top = jnp.max(top, 0, keepdims=True)
    c = math.log2(math.e) / math.sqrt(HEAD)
    for j in range(len(blocks)):
        rows = slice(j * tokens, (j + 1) * tokens)
        p = jnp.exp2((s_ref[rows, :] - top) * c)
        s_ref[rows, :] = p
        p_ref[rows, :] = p.astype(BF)
    lane = lax.broadcasted_iota(jnp.int32, (tokens, HEAD), 1)
    for pair in range(GROUP // 2):
        ot = mm(vat[...], p_ref[:, pair * 2 * tokens : (pair + 1) * 2 * tokens])
        for u in range(2):
            h = 2 * pair + u
            o = ot[:, u * tokens : (u + 1) * tokens].T
            inv = 1.0 / o[:, HEAD:]
            out = o[:, :HEAD] * inv
            o_ref[:, h * HEAD : (h + 1) * HEAD] = out.astype(BF)
            tp = (t_ref[:, h * HEAD : (h + 1) * HEAD].astype(F32) * inv).astype(BF)
            delta = jnp.sum(tp.astype(F32) * out, 1, keepdims=True)
            hi = delta.astype(BF).astype(F32)
            rest = delta - hi
            mid = rest.astype(BF).astype(F32)
            lo = rest - mid
            ext = jnp.where(
                lane == 0, -hi, jnp.where(lane == 1, -mid, jnp.where(lane == 2, -lo, 0.0))
            )
            taug[h * tokens : (h + 1) * tokens, 0:HEAD] = tp
            taug[h * tokens : (h + 1) * tokens, HEAD : 2 * HEAD] = ext.astype(BF)
    scale = 1.0 / math.sqrt(HEAD)
    for j, (_, g, b) in enumerate(blocks):
        rows = slice(j * tokens, (j + 1) * tokens)
        out_rows = slice(b * tokens, (b + 1) * tokens)
        x = mm(vaug[rows, :], taug[...], NT)
        ds = (s_ref[rows, :] * x).astype(BF)
        dk = mm(ds, qaug[:, 0:HEAD]) * scale
        dv = mm(p_ref[rows, :], taug[:, 0:HEAD])
        g[out_rows, 0:HEAD] = dk.astype(g.dtype)
        g[out_rows, HEAD : 2 * HEAD] = dv.astype(g.dtype)


def attention(q, t, own, r1, r2, r3, docs, own_rows, side_rows):
    tokens = q.shape[0]
    kv = q.shape[1] // (GROUP * HEAD)
    keys = (own_rows + 3 * side_rows) * tokens
    rows_all = GROUP * tokens
    wide = pl.BlockSpec((tokens, rows_all), lambda g: (0, g))

    def part(k):
        return pl.BlockSpec((k * tokens, 2 * HEAD), lambda g: (0, g))

    return pl.pallas_call(
        functools.partial(attn_kernel, own_rows, side_rows),
        grid=(kv,),
        in_specs=[wide, wide, part(own_rows)]
        + [part(side_rows)] * 3
        + [pl.BlockSpec(docs.shape, lambda g: (0, 0))],
        out_specs=[wide, part(own_rows)] + [part(side_rows)] * 3,
        out_shape=[
            jax.ShapeDtypeStruct((tokens, kv * rows_all), BF),
            jax.ShapeDtypeStruct((own_rows * tokens, kv * 2 * HEAD), F32),
        ]
        + [jax.ShapeDtypeStruct((side_rows * tokens, kv * 2 * HEAD), BF)] * 3,
        scratch_shapes=[
            pltpu.VMEM((keys, 2 * HEAD), BF),
            pltpu.VMEM((keys, 2 * HEAD), BF),
            pltpu.VMEM((2 * HEAD, keys), BF),
            pltpu.VMEM((rows_all, 2 * HEAD), BF),
            pltpu.VMEM((rows_all, 2 * HEAD), BF),
            pltpu.VMEM((keys, rows_all), F32),
            pltpu.VMEM((keys, rows_all), BF),
        ],
        compiler_params=pltpu.CompilerParams(vmem_limit_bytes=50 << 20),
        cost_estimate=pl.CostEstimate(
            flops=kv * keys * rows_all * HEAD * 10,
            bytes_accessed=8 << 20,
            transcendentals=kv * keys * rows_all,
        ),
    )(q, t, own, r1, r2, r3, docs)


def along_z(x, d):
    n = lax.axis_size("cz")
    return lax.ppermute(x, "cz", [(i - d, i) for i in range(n) if 0 <= i - d < n])


def along_x(x, d):
    n = lax.axis_size("cx")
    return lax.ppermute(x, "cx", [((i - d) % n, i) for i in range(n)])


def sum_among(x, axes):
    n = math.prod(lax.axis_size(a) for a in axes)
    return lax.all_to_all(jnp.broadcast_to(x[None], (n,) + x.shape), axes, 0, 0)


def per_device(query, key, value, key_shift, value_shift, doc_ids, target):
    tokens = query.shape[1]
    kv_local = key.shape[2] // HEAD
    far_rows = 4
    where_x = lax.axis_index("cx")
    key_new = (key[0].astype(F32) + key_shift[0]).astype(BF)
    val_new = (value[0].astype(F32) + value_shift[0]).astype(BF)
    lanes = []
    for h in range(kv_local):
        lanes += [key_new[:, h * HEAD : (h + 1) * HEAD], val_new[:, h * HEAD : (h + 1) * HEAD]]
    kv = jnp.concatenate(lanes, 1)
    width = kv.shape[1]
    docs = (doc_ids[0] + 1).astype(BF)[None, :]
    tail = jnp.pad(docs, ((0, 7), (0, width - tokens)))
    row = [jnp.concatenate([kv, tail], 0)]
    for k in range(1, far_rows + 1):
        row.append(along_z(row[0], k))
    keys_of = [r[:tokens] for r in row]
    docs_of = [r[tokens : tokens + 1] for r in row]
    sides = []
    for d in (1, 2, 3):
        ahead = where_x + d < lax.axis_size("cx")
        first = jnp.where(ahead, keys_of[0], keys_of[4])
        first_doc = jnp.where(ahead, docs_of[0], docs_of[4])
        pad = jnp.zeros((4, width), BF)
        sent = jnp.concatenate(
            [first, keys_of[3], keys_of[2], keys_of[1], first_doc, docs_of[3], docs_of[2], docs_of[1], pad], 0
        )
        sides.append(along_x(sent, d))
    own = jnp.concatenate([keys_of[4], keys_of[3], keys_of[2], keys_of[1], keys_of[0]], 0)
    docs_all = jnp.concatenate(
        [docs_of[4], docs_of[3], docs_of[2], docs_of[1], docs_of[0]]
        + [s[4 * tokens : 4 * tokens + 4] for s in sides],
        0,
    )[:, :tokens].astype(F32)
    docs_all = jnp.pad(docs_all, ((0, 32 - docs_all.shape[0]), (0, 0)))
    attn, gown, g1, g2, g3 = attention(
        query[0], target[0], own, sides[0], sides[1], sides[2], docs_all, 5, 4
    )
    back = [along_x(g, -d) for d, g in ((1, g1), (2, g2), (3, g3))]

    def piece(x, i):
        return x[i * tokens : (i + 1) * tokens].astype(F32)

    total = [None] * 5
    for k in (1, 2, 3):
        total[k] = piece(gown, 4 - k) + sum(piece(b, 4 - k) for b in back)
    total[0] = piece(gown, 4)
    total[4] = piece(gown, 0)
    for d, b in zip((1, 2, 3), back):
        ahead = where_x + d < lax.axis_size("cx")
        total[0] = total[0] + jnp.where(ahead, piece(b, 0), 0.0)
        total[4] = total[4] + jnp.where(ahead, 0.0, piece(b, 0))
    grad = total[0]
    for k in range(1, far_rows + 1):
        grad = grad + along_z(total[k].astype(BF), -k).astype(F32)
    grad_key = jnp.concatenate(
        [grad[:, 2 * h * HEAD : (2 * h + 1) * HEAD] for h in range(kv_local)], 1
    )
    grad_val = jnp.concatenate(
        [grad[:, (2 * h + 1) * HEAD : (2 * h + 2) * HEAD] for h in range(kv_local)], 1
    )
    ks, vs = key_shift[0], value_shift[0]
    sums = jnp.stack(
        [
            jnp.sum(ks * ks, -1) + jnp.sum(vs * vs, -1),
            jnp.sum(ks * grad_key, -1) + jnp.sum(vs * grad_val, -1),
            jnp.sum(grad_key * grad_key, -1) + jnp.sum(grad_val * grad_val, -1),
        ]
    )
    n_dp, n_x, n_tp = lax.axis_size("dp"), lax.axis_size("cx"), lax.axis_size("tp")
    plane = sum_among(sums, ("dp", "cx", "tp"))
    near = jnp.sum(
        lax.dynamic_slice_in_dim(
            plane, (lax.axis_index("dp") * n_x + where_x) * n_tp, n_tp, 0
        ),
        0,
    )
    square = jnp.sum(plane[:, 2])
    overall = jnp.sum(sum_among(jnp.full((1, 128), square), ("cz",))[:, 0, 0])
    count = n_dp * tokens * n_x * lax.axis_size("cz") * 2 * KV_HEADS * HEAD
    rms = jnp.sqrt(overall / count + 1e-05)
    a = step_size / rms
    size_sq = jnp.maximum(near[0] + 2.0 * a * near[1] + a * a * near[2], 0.0)
    radius = radius_scale * math.sqrt(2 * KV_HEADS * HEAD)
    factor = jnp.minimum(1.0, radius / jnp.sqrt(size_sq + 1e-06))[:, None]
    return (
        attn[None],
        ((ks + a * grad_key) * factor)[None],
        ((vs + a * grad_val) * factor)[None],
    )


def solution(mesh):
    sizes = mesh.devices.shape
    inner = Mesh(
        mesh.devices.reshape(sizes[0], sizes[1] // 4, 4, sizes[2]), ("dp", "cz", "cx", "tp")
    )
    whole = P("dp", ("cz", "cx"), "tp")
    in_specs = (whole,) * 5 + (P("dp", ("cz", "cx")), whole)
    return jax.shard_map(
        per_device, mesh=inner, in_specs=in_specs, out_specs=(whole,) * 3, check_vma=False
    )
```

```python
import functools
import math

import jax
import jax.numpy as jnp
from jax import lax
from jax.experimental import pallas as pl
from jax.experimental.pallas import tpu as pltpu
from jax.sharding import Mesh
from jax.sharding import PartitionSpec as P

HEADS = 64
KV_HEADS = 8
HEAD = 128
GROUP = HEADS // KV_HEADS
DOC_MAX = 2048

step_size = 0.1
radius_scale = 0.13

BF = jnp.bfloat16
F32 = jnp.float32
NT = (((1,), (1,)), ((), ()))
NN = (((1,), (0,)), ((), ()))
FAR = -1e30
ROWS = 4
HEADS_AT_ONCE = 1


def mm(a, b, dims=NN):
    return lax.dot_general(a, b, dims, preferred_element_type=F32)


def attn_kernel(
    q_ref, t_ref, win_ref, own_ref, _, o_ref, gwin_ref, gown_ref,
    kaug, vaug, vat, qaug, taug, s_ref, p_ref,
):
    tokens = q_ref.shape[0]
    rows_all = GROUP * tokens
    blocks = []
    for x in range(win_ref.shape[0]):
        for b in range(ROWS):
            blocks.append((win_ref.at[x], gwin_ref.at[x], b * tokens, ROWS * tokens + 8 * b))
    blocks.append((own_ref, gown_ref, 0, tokens))
    docs = jnp.concatenate([src[d : d + 1, 0:tokens] for src, _, _, d in blocks], 0).astype(F32)
    docs_sq = jnp.concatenate([docs, jnp.zeros((tokens - docs.shape[0], tokens), F32)], 0)
    doc_cols = docs_sq.T
    doc_row = docs[len(blocks) - 1 :, :]
    i_key = lax.broadcasted_iota(jnp.int32, (tokens, tokens), 0)
    i_qry = lax.broadcasted_iota(jnp.int32, (tokens, tokens), 1)
    one = jnp.ones((tokens, HEAD), BF)
    for j, (src, _, b, _) in enumerate(blocks):
        rows = slice(j * tokens, (j + 1) * tokens)
        kaug[rows, 0:HEAD] = src[b : b + tokens, 0:HEAD]
        v = src[b : b + tokens, HEAD : 2 * HEAD]
        vaug[rows, 0:HEAD] = v
        vaug[rows, HEAD : 2 * HEAD] = one
        vat[0:HEAD, rows] = v.T
        vat[HEAD : 2 * HEAD, rows] = one
        ok = doc_cols[:, j : j + 1] == doc_row
        if j == len(blocks) - 1:
            ok = ok & (i_key <= i_qry)
        kaug[rows, HEAD : HEAD + tokens] = jnp.where(ok, 0.0, FAR).astype(BF)
    eye = (i_key == i_qry).astype(F32).astype(BF)
    for h in range(GROUP):
        qaug[h * tokens : (h + 1) * tokens, 0:HEAD] = q_ref[:, h * HEAD : (h + 1) * HEAD]
        qaug[h * tokens : (h + 1) * tokens, HEAD : HEAD + tokens] = eye
    top = jnp.full((8, rows_all), -3e38, F32)
    for j in range(len(blocks)):
        rows = slice(j * tokens, (j + 1) * tokens)
        s = mm(kaug[rows, :], qaug[...], NT)
        s_ref[rows, :] = s
        top = jnp.maximum(top, jnp.max(s.reshape(tokens // 8, 8, rows_all), 0))
    top = jnp.max(top, 0, keepdims=True)
    c = math.log2(math.e) / math.sqrt(HEAD)
    for j in range(len(blocks)):
        rows = slice(j * tokens, (j + 1) * tokens)
        p = jnp.exp2((s_ref[rows, :] - top) * c)
        s_ref[rows, :] = p
        p_ref[rows, :] = p.astype(BF)
    lane = lax.broadcasted_iota(jnp.int32, (tokens, HEAD), 1)
    for pair in range(GROUP // 2):
        ot = mm(vat[...], p_ref[:, pair * 2 * tokens : (pair + 1) * 2 * tokens])
        for u in range(2):
            h = 2 * pair + u
            o = ot[:, u * tokens : (u + 1) * tokens].T
            inv = 1.0 / o[:, HEAD:]
            out = o[:, :HEAD] * inv
            o_ref[:, h * HEAD : (h + 1) * HEAD] = out.astype(BF)
            tp = (t_ref[:, h * HEAD : (h + 1) * HEAD].astype(F32) * inv).astype(BF)
            delta = jnp.sum(tp.astype(F32) * out, 1, keepdims=True)
            hi = delta.astype(BF).astype(F32)
            rest = delta - hi
            mid = rest.astype(BF).astype(F32)
            lo = rest - mid
            ext = jnp.where(
                lane == 0, -hi, jnp.where(lane == 1, -mid, jnp.where(lane == 2, -lo, 0.0))
            )
            taug[h * tokens : (h + 1) * tokens, 0:HEAD] = tp
            taug[h * tokens : (h + 1) * tokens, HEAD : 2 * HEAD] = ext.astype(BF)
    scale = 1.0 / math.sqrt(HEAD)
    for j, (_, g, b, _) in enumerate(blocks):
        rows = slice(j * tokens, (j + 1) * tokens)
        out_rows = slice(b, b + tokens)
        x = mm(vaug[rows, :], taug[...], NT)
        ds = (s_ref[rows, :] * x).astype(BF)
        dk = mm(ds, qaug[:, 0:HEAD]) * scale
        dv = mm(p_ref[rows, :], taug[:, 0:HEAD])
        g[out_rows, 0:HEAD] = dk.astype(g.dtype)
        g[out_rows, HEAD : 2 * HEAD] = dv.astype(g.dtype)


def attention(q, t, win, own, attn, first, heads):
    tokens = q.shape[0]
    n = win.shape[0]
    keys = (ROWS * n + 1) * tokens
    rows_all = GROUP * tokens
    wide = pl.BlockSpec((tokens, rows_all), lambda g: (0, g + first))

    def many(rows):
        return pl.BlockSpec((n, rows, 2 * HEAD), lambda g: (0, 0, g))

    def one(rows):
        return pl.BlockSpec((rows, 2 * HEAD), lambda g: (0, g))

    return pl.pallas_call(
        attn_kernel,
        grid=(heads,),
        in_specs=[wide, wide, many(win.shape[1]), one(own.shape[0]), pl.BlockSpec(memory_space=pl.ANY)],
        out_specs=[wide, many(ROWS * tokens), one(tokens)],
        out_shape=[
            jax.ShapeDtypeStruct(q.shape, BF),
            jax.ShapeDtypeStruct((n, ROWS * tokens, heads * 2 * HEAD), BF),
            jax.ShapeDtypeStruct((tokens, heads * 2 * HEAD), F32),
        ],
        input_output_aliases={4: 0} if first else {},
        scratch_shapes=[
            pltpu.VMEM((keys, 2 * HEAD), BF),
            pltpu.VMEM((keys, 2 * HEAD), BF),
            pltpu.VMEM((2 * HEAD, keys), BF),
            pltpu.VMEM((rows_all, 2 * HEAD), BF),
            pltpu.VMEM((rows_all, 2 * HEAD), BF),
            pltpu.VMEM((keys, rows_all), F32),
            pltpu.VMEM((keys, rows_all), BF),
        ],
        compiler_params=pltpu.CompilerParams(vmem_limit_bytes=40 << 20),
        cost_estimate=pl.CostEstimate(
            flops=heads * keys * rows_all * HEAD * 10,
            bytes_accessed=heads * 4 << 20,
            transcendentals=heads * keys * rows_all,
        ),
    )(q, t, win, own, attn)


def along_z(x, d):
    n = lax.axis_size("cz")
    return lax.ppermute(x, "cz", [(i - d, i) for i in range(n) if 0 <= i - d < n])


def swap_x(x):
    return lax.all_to_all(x, "cx", 0, 0)


def sum_among(x, axes):
    n = math.prod(lax.axis_size(a) for a in axes)
    return lax.all_to_all(jnp.broadcast_to(x[None], (n,) + x.shape), axes, 0, 0)


def per_device(query, key, value, key_shift, value_shift, doc_ids, target):
    tokens = query.shape[1]
    kv_local = key.shape[2] // HEAD
    where_x = lax.axis_index("cx")
    n_x = lax.axis_size("cx")
    key_new = (key[0].astype(F32) + key_shift[0]).astype(BF)
    val_new = (value[0].astype(F32) + value_shift[0]).astype(BF)
    docs = (doc_ids[0] + 1).astype(BF)[None, :]
    later = jnp.arange(n_x)[:, None, None] > where_x
    own, wins = [], []
    for h in range(0, kv_local, HEADS_AT_ONCE):
        lanes = []
        for i in range(h, h + HEADS_AT_ONCE):
            part = slice(i * HEAD, (i + 1) * HEAD)
            lanes += [key_new[:, part], val_new[:, part]]
        kv = jnp.concatenate(lanes, 1)
        tail = jnp.pad(docs, ((0, 7), (0, kv.shape[1] - tokens)))
        row = jnp.concatenate([kv, tail], 0)
        one, two = along_z(row, 1), along_z(row, 2)
        near = jnp.concatenate([one[:tokens], two[:tokens], one[tokens:], two[tokens:]], 0)
        far = along_z(near, 2)
        keep = 2 * tokens
        mixed = jnp.where(later, row[None, :tokens], far[None, tokens:keep])
        mixed_docs = jnp.where(later, row[None, tokens:], far[None, keep + 8 :])

        def each(x):
            return jnp.broadcast_to(x[None], (n_x,) + x.shape)

        sent = jnp.concatenate(
            [mixed, each(near[:keep]), each(far[:tokens]), mixed_docs, each(near[keep:]), each(far[keep : keep + 8])], 1
        )
        own.append(row)
        wins.append(swap_x(sent))
    attn = query[0]
    grads = []
    for i, h in enumerate(range(0, kv_local, HEADS_AT_ONCE)):
        attn, gwin, gown = attention(query[0], target[0], wins[i], own[i], attn, h, HEADS_AT_ONCE)
        back = swap_x(gwin)

        def piece(b):
            return back[:, b * tokens : (b + 1) * tokens].astype(F32)

        part0 = gown + jnp.sum(jnp.where(later, piece(0), 0.0), 0)
        part4 = jnp.sum(jnp.where(later, 0.0, piece(0)), 0)
        part3 = jnp.sum(piece(3), 0)
        far = along_z(jnp.concatenate([part3, part4], 0).astype(BF), -2).astype(F32)
        part1 = jnp.sum(piece(1), 0) + far[:tokens]
        part2 = jnp.sum(piece(2), 0) + far[tokens:]
        two = along_z(part2.astype(BF), -2)
        one = along_z(part1.astype(BF), -1)
        grads.append(part0 + two.astype(F32) + one.astype(F32))
    grad = jnp.concatenate(grads, 1)
    grad_key = jnp.concatenate(
        [grad[:, 2 * h * HEAD : (2 * h + 1) * HEAD] for h in range(kv_local)], 1
    )
    grad_val = jnp.concatenate(
        [grad[:, (2 * h + 1) * HEAD : (2 * h + 2) * HEAD] for h in range(kv_local)], 1
    )
    ks, vs = key_shift[0], value_shift[0]
    sums = jnp.stack(
        [
            jnp.sum(ks * ks, -1) + jnp.sum(vs * vs, -1),
            jnp.sum(ks * grad_key, -1) + jnp.sum(vs * grad_val, -1),
            jnp.sum(grad_key * grad_key, -1) + jnp.sum(grad_val * grad_val, -1),
        ]
    )
    n_dp, n_tp = lax.axis_size("dp"), lax.axis_size("tp")
    plane = sum_among(sums, ("dp", "cx", "tp"))
    near = jnp.sum(
        lax.dynamic_slice_in_dim(
            plane, (lax.axis_index("dp") * n_x + where_x) * n_tp, n_tp, 0
        ),
        0,
    )
    square = jnp.sum(plane[:, 2])
    overall = jnp.sum(sum_among(jnp.full((1, 128), square), ("cz",))[:, 0, 0])
    count = n_dp * tokens * n_x * lax.axis_size("cz") * 2 * KV_HEADS * HEAD
    rms = jnp.sqrt(overall / count + 1e-05)
    a = step_size / rms
    size_sq = jnp.maximum(near[0] + 2.0 * a * near[1] + a * a * near[2], 0.0)
    radius = radius_scale * math.sqrt(2 * KV_HEADS * HEAD)
    factor = jnp.minimum(1.0, radius / jnp.sqrt(size_sq + 1e-06))[:, None]
    return (
        attn[None],
        ((ks + a * grad_key) * factor)[None],
        ((vs + a * grad_val) * factor)[None],
    )


def solution(mesh):
    sizes = mesh.devices.shape
    inner = Mesh(
        mesh.devices.reshape(sizes[0], sizes[1] // 4, 4, sizes[2]), ("dp", "cz", "cx", "tp")
    )
    whole = P("dp", ("cz", "cx"), "tp")
    in_specs = (whole,) * 5 + (P("dp", ("cz", "cx")), whole)
    return jax.shard_map(
        per_device, mesh=inner, in_specs=in_specs, out_specs=(whole,) * 3, check_vma=False
    )
```

```python
import functools
import math

import jax
import jax.numpy as jnp
from jax import lax
from jax.experimental import pallas as pl
from jax.experimental.pallas import tpu as pltpu
from jax.sharding import Mesh
from jax.sharding import PartitionSpec as P

HEADS = 64
KV_HEADS = 8
HEAD = 128
GROUP = HEADS // KV_HEADS
DOC_MAX = 2048

step_size = 0.1
radius_scale = 0.13

BF = jnp.bfloat16
F32 = jnp.float32
NT = (((1,), (1,)), ((), ()))
NN = (((1,), (0,)), ((), ()))
FAR = -1e30
ROWS = 4
TAIL = 8


def mm(a, b, dims=NN):
    return lax.dot_general(a, b, dims, preferred_element_type=F32)


def attn_kernel(
    q_ref, t_ref, win_ref, own_ref, _, o_ref, gwin_ref, gown_ref,
    kaug, vaug, vat, qaug, taug, s_ref, p_ref,
):
    tokens = q_ref.shape[0]
    rows_all = GROUP * tokens
    blocks = []
    for x in range(win_ref.shape[0]):
        for b in range(ROWS):
            blocks.append((win_ref.at[x], gwin_ref.at[x], b))
    blocks.append((own_ref, gown_ref, 0))
    step = tokens + TAIL
    docs = jnp.concatenate(
        [src[b * step + tokens : b * step + tokens + 1, 0:tokens].astype(F32) for src, _, b in blocks], 0
    )
    docs_sq = jnp.concatenate([docs, jnp.zeros((tokens - docs.shape[0], tokens), F32)], 0)
    doc_cols = docs_sq.T
    doc_row = docs[len(blocks) - 1 :, :]
    i_key = lax.broadcasted_iota(jnp.int32, (tokens, tokens), 0)
    i_qry = lax.broadcasted_iota(jnp.int32, (tokens, tokens), 1)
    one = jnp.ones((tokens, HEAD), BF)
    for j, (src, _, b) in enumerate(blocks):
        rows = slice(j * tokens, (j + 1) * tokens)
        kaug[rows, 0:HEAD] = src[b * step : b * step + tokens, 0:HEAD]
        v = src[b * step : b * step + tokens, HEAD : 2 * HEAD]
        vaug[rows, 0:HEAD] = v
        vaug[rows, HEAD : 2 * HEAD] = one
        vat[0:HEAD, rows] = v.T
        vat[HEAD : 2 * HEAD, rows] = one
        ok = doc_cols[:, j : j + 1] == doc_row
        if j == len(blocks) - 1:
            ok = ok & (i_key <= i_qry)
        kaug[rows, HEAD : HEAD + tokens] = jnp.where(ok, 0.0, FAR).astype(BF)
    eye = (i_key == i_qry).astype(F32).astype(BF)
    for h in range(GROUP):
        qaug[h * tokens : (h + 1) * tokens, 0:HEAD] = q_ref[:, h * HEAD : (h + 1) * HEAD]
        qaug[h * tokens : (h + 1) * tokens, HEAD : HEAD + tokens] = eye
    top = jnp.full((8, rows_all), -3e38, F32)
    for j in range(len(blocks)):
        rows = slice(j * tokens, (j + 1) * tokens)
        s = mm(kaug[rows, :], qaug[...], NT)
        s_ref[rows, :] = s
        top = jnp.maximum(top, jnp.max(s.reshape(tokens // 8, 8, rows_all), 0))
    top = jnp.max(top, 0, keepdims=True)
    c = math.log2(math.e) / math.sqrt(HEAD)
    for j in range(len(blocks)):
        rows = slice(j * tokens, (j + 1) * tokens)
        p = jnp.exp2((s_ref[rows, :] - top) * c)
        s_ref[rows, :] = p
        p_ref[rows, :] = p.astype(BF)
    lane = lax.broadcasted_iota(jnp.int32, (tokens, HEAD), 1)
    for pair in range(GROUP // 2):
        ot = mm(vat[...], p_ref[:, pair * 2 * tokens : (pair + 1) * 2 * tokens])
        for u in range(2):
            h = 2 * pair + u
            o = ot[:, u * tokens : (u + 1) * tokens].T
            inv = 1.0 / o[:, HEAD:]
            out = o[:, :HEAD] * inv
            o_ref[:, h * HEAD : (h + 1) * HEAD] = out.astype(BF)
            tp = (t_ref[:, h * HEAD : (h + 1) * HEAD].astype(F32) * inv).astype(BF)
            delta = jnp.sum(tp.astype(F32) * out, 1, keepdims=True)
            hi = delta.astype(BF).astype(F32)
            rest = delta - hi
            mid = rest.astype(BF).astype(F32)
            lo = rest - mid
            ext = jnp.where(
                lane == 0, -hi, jnp.where(lane == 1, -mid, jnp.where(lane == 2, -lo, 0.0))
            )
            taug[h * tokens : (h + 1) * tokens, 0:HEAD] = tp
            taug[h * tokens : (h + 1) * tokens, HEAD : 2 * HEAD] = ext.astype(BF)
    scale = 1.0 / math.sqrt(HEAD)
    for j, (_, g, b) in enumerate(blocks):
        rows = slice(j * tokens, (j + 1) * tokens)
        out_rows = slice(b * tokens, (b + 1) * tokens)
        x = mm(vaug[rows, :], taug[...], NT)
        ds = (s_ref[rows, :] * x).astype(BF)
        dk = mm(ds, qaug[:, 0:HEAD]) * scale
        dv = mm(p_ref[rows, :], taug[:, 0:HEAD])
        g[out_rows, 0:HEAD] = dk.astype(g.dtype)
        g[out_rows, HEAD : 2 * HEAD] = dv.astype(g.dtype)


def attention(q, t, win, own, attn, head):
    tokens = q.shape[0]
    n = win.shape[0]
    keys = (ROWS * n + 1) * tokens
    rows_all = GROUP * tokens
    wide = pl.BlockSpec((tokens, rows_all), lambda g: (0, head))
    whole = pl.BlockSpec(memory_space=pltpu.VMEM)
    return pl.pallas_call(
        attn_kernel,
        grid=(1,),
        in_specs=[
            wide,
            wide,
            whole,
            pl.BlockSpec((own.shape[0], 2 * HEAD), lambda g: (0, head)),
            pl.BlockSpec(memory_space=pl.ANY),
        ],
        out_specs=[wide, whole, whole],
        out_shape=[
            jax.ShapeDtypeStruct(q.shape, BF),
            jax.ShapeDtypeStruct((n, ROWS * tokens, 2 * HEAD), BF),
            jax.ShapeDtypeStruct((tokens, 2 * HEAD), F32),
        ],
        input_output_aliases={4: 0} if head else {},
        scratch_shapes=[
            pltpu.VMEM((keys, 2 * HEAD), BF),
            pltpu.VMEM((keys, 2 * HEAD), BF),
            pltpu.VMEM((2 * HEAD, keys), BF),
            pltpu.VMEM((rows_all, 2 * HEAD), BF),
            pltpu.VMEM((rows_all, 2 * HEAD), BF),
            pltpu.VMEM((keys, rows_all), F32),
            pltpu.VMEM((keys, rows_all), BF),
        ],
        compiler_params=pltpu.CompilerParams(vmem_limit_bytes=32 << 20),
        cost_estimate=pl.CostEstimate(
            flops=keys * rows_all * HEAD * 10,
            bytes_accessed=4 << 20,
            transcendentals=keys * rows_all,
        ),
    )(q, t, win, own, attn)


def prepare_kernel(k_ref, v_ref, ks_ref, vs_ref, docs_ref, row_ref):
    tokens = k_ref.shape[0]
    k = (k_ref[...].astype(F32) + ks_ref[...]).astype(BF)
    v = (v_ref[...].astype(F32) + vs_ref[...]).astype(BF)
    docs = (docs_ref[...] + 1).astype(F32)
    docs = jnp.broadcast_to(docs, (TAIL, docs.shape[1])).astype(BF)
    for h in range(k.shape[1] // HEAD):
        at = 2 * h * HEAD
        row_ref[0:tokens, at : at + HEAD] = k[:, h * HEAD : (h + 1) * HEAD]
        row_ref[0:tokens, at + HEAD : at + 2 * HEAD] = v[:, h * HEAD : (h + 1) * HEAD]
        row_ref[tokens:, at : at + tokens] = docs
        row_ref[tokens:, at + HEAD : at + HEAD + tokens] = docs


def prepare(k, v, ks, vs, docs):
    tokens, width = k.shape
    return pl.pallas_call(
        prepare_kernel,
        out_shape=jax.ShapeDtypeStruct((tokens + TAIL, 2 * width), BF),
        compiler_params=pltpu.CompilerParams(vmem_limit_bytes=4 << 20),
        cost_estimate=pl.CostEstimate(flops=1 << 17, bytes_accessed=1 << 19, transcendentals=0),
    )(k, v, ks, vs, docs)


def spread_kernel(x_ref, row_ref, near_ref, far_ref, out_ref):
    rows = row_ref.shape[0]
    target = pl.program_id(0)

    @pl.when(target > x_ref[0])
    def _():
        out_ref[0, 0:rows, :] = row_ref[...]

    @pl.when(target <= x_ref[0])
    def _():
        out_ref[0, 0:rows, :] = far_ref[rows:, :]

    out_ref[0, rows : 3 * rows, :] = near_ref[...]
    out_ref[0, 3 * rows :, :] = far_ref[0:rows, :]


def spread(where_x, row, near, far, head, n):
    rows, width = near.shape
    return pl.pallas_call(
        spread_kernel,
        grid_spec=pltpu.PrefetchScalarGridSpec(
            num_scalar_prefetch=1,
            grid=(n,),
            in_specs=[
                pl.BlockSpec((rows // 2, width), lambda g, x: (0, head)),
                pl.BlockSpec((rows, width), lambda g, x: (0, 0)),
                pl.BlockSpec((rows, width), lambda g, x: (0, 0)),
            ],
            out_specs=pl.BlockSpec((1, 2 * rows, width), lambda g, x: (g, 0, 0)),
        ),
        out_shape=jax.ShapeDtypeStruct((n, 2 * rows, width), BF),
        compiler_params=pltpu.CompilerParams(vmem_limit_bytes=8 << 20),
        cost_estimate=pl.CostEstimate(flops=0, bytes_accessed=2 << 20, transcendentals=0),
    )(where_x, row, near, far)


def fold_kernel(x_ref, back_ref, gown_ref, sent_ref, kept_ref):
    tokens = gown_ref.shape[0]
    n = back_ref.shape[0]

    def part(i, b):
        return back_ref[i, b * tokens : (b + 1) * tokens, :].astype(F32)

    own = gown_ref[...]
    last = jnp.zeros_like(own)
    for i in range(n):
        later = i > x_ref[0]
        p = part(i, 0)
        own = own + jnp.where(later, p, 0.0)
        last = last + jnp.where(later, 0.0, p)
    kept_ref[0:tokens, :] = own
    for b in (1, 2):
        kept_ref[b * tokens : (b + 1) * tokens, :] = sum(part(i, b) for i in range(n))
    sent_ref[0:tokens, :] = sum(part(i, 3) for i in range(n)).astype(BF)
    sent_ref[tokens:, :] = last.astype(BF)


def fold(where_x, back, gown):
    tokens, width = gown.shape
    vmem = pl.BlockSpec(memory_space=pltpu.VMEM)
    return pl.pallas_call(
        fold_kernel,
        in_specs=[pl.BlockSpec(memory_space=pltpu.SMEM), vmem, vmem],
        out_specs=[vmem, vmem],
        out_shape=[
            jax.ShapeDtypeStruct((2 * tokens, width), BF),
            jax.ShapeDtypeStruct((3 * tokens, width), F32),
        ],
        compiler_params=pltpu.CompilerParams(vmem_limit_bytes=8 << 20),
        cost_estimate=pl.CostEstimate(flops=1 << 19, bytes_accessed=2 << 20, transcendentals=0),
    )(where_x, back, gown)


def along_z(x, d):
    n = lax.axis_size("cz")
    return lax.ppermute(x, "cz", [(i - d, i) for i in range(n) if 0 <= i - d < n])


def swap_x(x):
    return lax.all_to_all(x, "cx", 0, 0)


def sum_among(x, axes):
    n = math.prod(lax.axis_size(a) for a in axes)
    return lax.all_to_all(jnp.broadcast_to(x[None], (n,) + x.shape), axes, 0, 0)


def per_device(query, key, value, key_shift, value_shift, doc_ids, target):
    tokens = query.shape[1]
    kv_local = key.shape[2] // HEAD
    where_x = lax.axis_index("cx")
    n_x = lax.axis_size("cx")
    at_x = where_x.astype(jnp.int32)[None]
    row = prepare(key[0], value[0], key_shift[0], value_shift[0], doc_ids)
    one, two = along_z(row, 1), along_z(row, 2)
    wins = []
    for h in range(kv_local):
        part = slice(2 * h * HEAD, 2 * (h + 1) * HEAD)
        near = jnp.concatenate([one[:, part], two[:, part]], 0)
        far = along_z(near, 2)
        wins.append(swap_x(spread(at_x, row, near, far, h, n_x)))
    attn = query[0]
    kept = []
    for h in range(kv_local):
        attn, gwin, gown = attention(query[0], target[0], wins[h], row, attn, h)
        sent, mine = fold(at_x, swap_x(gwin), gown)
        kept.append((along_z(sent, -2), mine))
    near = [
        jnp.concatenate(
            [
                (mine[(b + 1) * tokens : (b + 2) * tokens] + far[b * tokens : (b + 1) * tokens]).astype(BF)
                for far, mine in kept
            ],
            1,
        )
        for b in range(2)
    ]
    two, one = along_z(near[1], -2), along_z(near[0], -1)
    grad = jnp.concatenate([mine[:tokens] for _, mine in kept], 1) + one.astype(F32) + two.astype(F32)
    grad_key = jnp.concatenate(
        [grad[:, 2 * h * HEAD : (2 * h + 1) * HEAD] for h in range(kv_local)], 1
    )
    grad_val = jnp.concatenate(
        [grad[:, (2 * h + 1) * HEAD : (2 * h + 2) * HEAD] for h in range(kv_local)], 1
    )
    ks, vs = key_shift[0], value_shift[0]
    sums = jnp.stack(
        [
            jnp.sum(ks * ks, -1) + jnp.sum(vs * vs, -1),
            jnp.sum(ks * grad_key, -1) + jnp.sum(vs * grad_val, -1),
            jnp.sum(grad_key * grad_key, -1) + jnp.sum(grad_val * grad_val, -1),
        ]
    )
    n_dp, n_tp = lax.axis_size("dp"), lax.axis_size("tp")
    plane = sum_among(sums, ("dp", "cx", "tp"))
    near = jnp.sum(
        lax.dynamic_slice_in_dim(
            plane, (lax.axis_index("dp") * n_x + where_x) * n_tp, n_tp, 0
        ),
        0,
    )
    square = jnp.sum(plane[:, 2])
    overall = jnp.sum(sum_among(jnp.full((1, 128), square), ("cz",))[:, 0, 0])
    count = n_dp * tokens * n_x * lax.axis_size("cz") * 2 * KV_HEADS * HEAD
    rms = jnp.sqrt(overall / count + 1e-05)
    a = step_size / rms
    size_sq = jnp.maximum(near[0] + 2.0 * a * near[1] + a * a * near[2], 0.0)
    radius = radius_scale * math.sqrt(2 * KV_HEADS * HEAD)
    factor = jnp.minimum(1.0, radius / jnp.sqrt(size_sq + 1e-06))[:, None]
    return (
        attn[None],
        ((ks + a * grad_key) * factor)[None],
        ((vs + a * grad_val) * factor)[None],
    )


def solution(mesh):
    sizes = mesh.devices.shape
    inner = Mesh(
        mesh.devices.reshape(sizes[0], sizes[1] // 4, 4, sizes[2]), ("dp", "cz", "cx", "tp")
    )
    whole = P("dp", ("cz", "cx"), "tp")
    in_specs = (whole,) * 5 + (P("dp", ("cz", "cx")), whole)
    return jax.shard_map(
        per_device, mesh=inner, in_specs=in_specs, out_specs=(whole,) * 3, check_vma=False
    )
```

```python
import functools
import math

import jax
import jax.numpy as jnp
from jax import lax
from jax.experimental import pallas as pl
from jax.experimental.pallas import tpu as pltpu
from jax.sharding import Mesh
from jax.sharding import PartitionSpec as P

HEADS = 64
KV_HEADS = 8
HEAD = 128
GROUP = HEADS // KV_HEADS
DOC_MAX = 2048

step_size = 0.1
radius_scale = 0.13

BF = jnp.bfloat16
F32 = jnp.float32
NT = (((1,), (1,)), ((), ()))
NN = (((1,), (0,)), ((), ()))
FAR = -1e30
ROWS = 4
TAIL = 8


def mm(a, b, dims=NN):
    return lax.dot_general(a, b, dims, preferred_element_type=F32)


def attn_kernel(
    q_ref, t_ref, win_ref, own_ref, _, o_ref, gwin_ref, gown_ref,
    kaug, vaug, vat, qaug, taug, s_ref, p_ref,
):
    tokens = q_ref.shape[0]
    rows_all = GROUP * tokens
    blocks = []
    for x in range(win_ref.shape[0]):
        for b in range(ROWS):
            blocks.append((win_ref.at[x], gwin_ref.at[x], b))
    blocks.append((own_ref, gown_ref, 0))
    step = tokens + TAIL
    docs = jnp.concatenate(
        [src[b * step + tokens : b * step + tokens + 1, 0:tokens].astype(F32) for src, _, b in blocks], 0
    )
    docs_sq = jnp.concatenate([docs, jnp.zeros((tokens - docs.shape[0], tokens), F32)], 0)
    doc_cols = docs_sq.T
    doc_row = docs[len(blocks) - 1 :, :]
    i_key = lax.broadcasted_iota(jnp.int32, (tokens, tokens), 0)
    i_qry = lax.broadcasted_iota(jnp.int32, (tokens, tokens), 1)
    one = jnp.ones((tokens, HEAD), BF)
    for j, (src, _, b) in enumerate(blocks):
        rows = slice(j * tokens, (j + 1) * tokens)
        kaug[rows, 0:HEAD] = src[b * step : b * step + tokens, 0:HEAD]
        v = src[b * step : b * step + tokens, HEAD : 2 * HEAD]
        vaug[rows, 0:HEAD] = v
        vaug[rows, HEAD : 2 * HEAD] = one
        vat[0:HEAD, rows] = v.T
        vat[HEAD : 2 * HEAD, rows] = one
        ok = doc_cols[:, j : j + 1] == doc_row
        if j == len(blocks) - 1:
            ok = ok & (i_key <= i_qry)
        kaug[rows, HEAD : HEAD + tokens] = jnp.where(ok, 0.0, FAR).astype(BF)
    eye = (i_key == i_qry).astype(F32).astype(BF)
    for h in range(GROUP):
        qaug[h * tokens : (h + 1) * tokens, 0:HEAD] = q_ref[:, h * HEAD : (h + 1) * HEAD]
        qaug[h * tokens : (h + 1) * tokens, HEAD : HEAD + tokens] = eye
    scores = mm(kaug[...], qaug[...], NT)
    s_ref[...] = scores
    top = jnp.max(scores.reshape(scores.shape[0] // 8, 8, rows_all), 0)
    top = jnp.max(top, 0, keepdims=True)
    c = math.log2(math.e) / math.sqrt(HEAD)
    for j in range(len(blocks)):
        rows = slice(j * tokens, (j + 1) * tokens)
        p_ref[rows, :] = jnp.exp2((s_ref[rows, :] - top) * c).astype(BF)
    lane = lax.broadcasted_iota(jnp.int32, (tokens, HEAD), 1)
    for pair in range(GROUP // 2):
        ot = mm(vat[...], p_ref[:, pair * 2 * tokens : (pair + 1) * 2 * tokens])
        for u in range(2):
            h = 2 * pair + u
            o = ot[:, u * tokens : (u + 1) * tokens].T
            inv = 1.0 / o[:, HEAD:]
            out = o[:, :HEAD] * inv
            o_ref[:, h * HEAD : (h + 1) * HEAD] = out.astype(BF)
            tp = (t_ref[:, h * HEAD : (h + 1) * HEAD].astype(F32) * inv).astype(BF)
            delta = jnp.sum(tp.astype(F32) * out, 1, keepdims=True)
            hi = delta.astype(BF).astype(F32)
            rest = delta - hi
            mid = rest.astype(BF).astype(F32)
            lo = rest - mid
            ext = jnp.where(
                lane == 0, -hi, jnp.where(lane == 1, -mid, jnp.where(lane == 2, -lo, 0.0))
            )
            taug[h * tokens : (h + 1) * tokens, 0:HEAD] = tp
            taug[h * tokens : (h + 1) * tokens, HEAD : 2 * HEAD] = ext.astype(BF)
    scale = 1.0 / math.sqrt(HEAD)
    ds = (p_ref[...].astype(F32) * mm(vaug[...], taug[...], NT)).astype(BF)
    dk = mm(ds, qaug[:, 0:HEAD]) * scale
    dv = mm(p_ref[...], taug[:, 0:HEAD])
    for j, (_, g, b) in enumerate(blocks):
        rows = slice(j * tokens, (j + 1) * tokens)
        out_rows = slice(b * tokens, (b + 1) * tokens)
        g[out_rows, 0:HEAD] = dk[rows].astype(g.dtype)
        g[out_rows, HEAD : 2 * HEAD] = dv[rows].astype(g.dtype)


def attention(q, t, win, own, attn, head):
    tokens = q.shape[0]
    n = win.shape[0]
    keys = (ROWS * n + 1) * tokens
    rows_all = GROUP * tokens
    wide = pl.BlockSpec((tokens, rows_all), lambda g: (0, head))
    whole = pl.BlockSpec(memory_space=pltpu.VMEM)
    return pl.pallas_call(
        attn_kernel,
        grid=(1,),
        in_specs=[
            wide,
            wide,
            whole,
            pl.BlockSpec((own.shape[0], 2 * HEAD), lambda g: (0, head)),
            pl.BlockSpec(memory_space=pl.ANY),
        ],
        out_specs=[wide, whole, whole],
        out_shape=[
            jax.ShapeDtypeStruct(q.shape, BF),
            jax.ShapeDtypeStruct((n, ROWS * tokens, 2 * HEAD), BF),
            jax.ShapeDtypeStruct((tokens, 2 * HEAD), F32),
        ],
        input_output_aliases={4: 0} if head else {},
        scratch_shapes=[
            pltpu.VMEM((keys, 2 * HEAD), BF),
            pltpu.VMEM((keys, 2 * HEAD), BF),
            pltpu.VMEM((2 * HEAD, keys), BF),
            pltpu.VMEM((rows_all, 2 * HEAD), BF),
            pltpu.VMEM((rows_all, 2 * HEAD), BF),
            pltpu.VMEM((keys, rows_all), F32),
            pltpu.VMEM((keys, rows_all), BF),
        ],
        compiler_params=pltpu.CompilerParams(vmem_limit_bytes=32 << 20),
        cost_estimate=pl.CostEstimate(
            flops=keys * rows_all * HEAD * 10,
            bytes_accessed=4 << 20,
            transcendentals=keys * rows_all,
        ),
    )(
        pltpu.with_memory_space_constraint(q, pltpu.HBM),
        pltpu.with_memory_space_constraint(t, pltpu.HBM),
        win,
        own,
        attn,
    )


def prepare_kernel(k_ref, v_ref, ks_ref, vs_ref, docs_ref, row_ref):
    tokens = k_ref.shape[0]
    k = (k_ref[...].astype(F32) + ks_ref[...]).astype(BF)
    v = (v_ref[...].astype(F32) + vs_ref[...]).astype(BF)
    docs = (docs_ref[...] + 1).astype(F32)
    docs = jnp.broadcast_to(docs, (TAIL, docs.shape[1])).astype(BF)
    for h in range(k.shape[1] // HEAD):
        at = 2 * h * HEAD
        row_ref[0:tokens, at : at + HEAD] = k[:, h * HEAD : (h + 1) * HEAD]
        row_ref[0:tokens, at + HEAD : at + 2 * HEAD] = v[:, h * HEAD : (h + 1) * HEAD]
        row_ref[tokens:, at : at + tokens] = docs
        row_ref[tokens:, at + HEAD : at + HEAD + tokens] = docs


def prepare(k, v, ks, vs, docs):
    tokens, width = k.shape
    return pl.pallas_call(
        prepare_kernel,
        out_shape=jax.ShapeDtypeStruct((tokens + TAIL, 2 * width), BF),
        cost_estimate=pl.CostEstimate(flops=1 << 17, bytes_accessed=1 << 19, transcendentals=0),
    )(k, v, ks, vs, docs)


def spread_kernel(x_ref, row_ref, near_ref, far_ref, out_ref):
    rows = row_ref.shape[0]
    for i in range(out_ref.shape[0]):
        @pl.when(i > x_ref[0])
        def _():
            out_ref[i, 0:rows, :] = row_ref[...]

        @pl.when(i <= x_ref[0])
        def _():
            out_ref[i, 0:rows, :] = far_ref[rows:, :]

        out_ref[i, rows : 3 * rows, :] = near_ref[...]
        out_ref[i, 3 * rows :, :] = far_ref[0:rows, :]


def spread(where_x, row, near, far, head, n):
    rows, width = near.shape
    whole = pl.BlockSpec(memory_space=pltpu.VMEM)
    return pl.pallas_call(
        spread_kernel,
        grid=(1,),
        in_specs=[
            pl.BlockSpec(memory_space=pltpu.SMEM),
            pl.BlockSpec((rows // 2, width), lambda g: (0, head)),
            whole,
            whole,
        ],
        out_specs=whole,
        out_shape=jax.ShapeDtypeStruct((n, 2 * rows, width), BF),
        compiler_params=pltpu.CompilerParams(vmem_limit_bytes=8 << 20),
        cost_estimate=pl.CostEstimate(flops=0, bytes_accessed=2 << 20, transcendentals=0),
    )(where_x, row, near, far)


def fold_kernel(x_ref, back_ref, gown_ref, sent_ref, kept_ref):
    tokens = gown_ref.shape[0]
    n = back_ref.shape[0]

    def part(i, b):
        return back_ref[i, b * tokens : (b + 1) * tokens, :].astype(F32)

    own = gown_ref[...]
    last = jnp.zeros_like(own)
    for i in range(n):
        later = i > x_ref[0]
        p = part(i, 0)
        own = own + jnp.where(later, p, 0.0)
        last = last + jnp.where(later, 0.0, p)
    kept_ref[0:tokens, :] = own
    for b in (1, 2):
        kept_ref[b * tokens : (b + 1) * tokens, :] = sum(part(i, b) for i in range(n))
    sent_ref[0:tokens, :] = sum(part(i, 3) for i in range(n)).astype(BF)
    sent_ref[tokens:, :] = last.astype(BF)


def fold(where_x, back, gown):
    tokens, width = gown.shape
    vmem = pl.BlockSpec(memory_space=pltpu.VMEM)
    return pl.pallas_call(
        fold_kernel,
        in_specs=[pl.BlockSpec(memory_space=pltpu.SMEM), vmem, vmem],
        out_specs=[vmem, vmem],
        out_shape=[
            jax.ShapeDtypeStruct((2 * tokens, width), BF),
            jax.ShapeDtypeStruct((3 * tokens, width), F32),
        ],
        compiler_params=pltpu.CompilerParams(vmem_limit_bytes=8 << 20),
        cost_estimate=pl.CostEstimate(flops=1 << 19, bytes_accessed=2 << 20, transcendentals=0),
    )(where_x, back, gown)


def gather_kernel(n_tp, first_ref, plane_ref, near_ref, out_ref):
    square = jnp.sum(plane_ref[:, 2, :])
    out_ref[...] = jnp.full(out_ref.shape, square, F32)
    near_ref[...] = jnp.sum(plane_ref[pl.ds(first_ref[0], n_tp)], 0)


def gather(first, plane, n, n_tp):
    vmem = pl.BlockSpec(memory_space=pltpu.VMEM)
    return pl.pallas_call(
        functools.partial(gather_kernel, n_tp),
        in_specs=[pl.BlockSpec(memory_space=pltpu.SMEM), vmem],
        out_specs=[vmem, vmem],
        out_shape=[
            jax.ShapeDtypeStruct(plane.shape[1:], F32),
            jax.ShapeDtypeStruct((n, 1, plane.shape[2]), F32),
        ],
        compiler_params=pltpu.CompilerParams(vmem_limit_bytes=4 << 20),
        cost_estimate=pl.CostEstimate(flops=1 << 14, bytes_accessed=1 << 16, transcendentals=0),
    )(first, plane)


def update_kernel(count, all_ref, near_ref, ks_ref, vs_ref, grad_ref, nk_ref, nv_ref):
    tokens = ks_ref.shape[0]
    overall = jnp.sum(all_ref[...], 0)
    a = step_size / jnp.sqrt(overall / count + 1e-05)
    near = near_ref[...]
    size_sq = jnp.maximum(near[0:1] + 2.0 * a * near[1:2] + a * a * near[2:3], 0.0)
    radius = radius_scale * math.sqrt(2 * KV_HEADS * HEAD)
    factor = jnp.minimum(1.0, radius / jnp.sqrt(size_sq + 1e-06))
    factor = jnp.broadcast_to(factor, (tokens, tokens)).T
    for h in range(ks_ref.shape[1] // HEAD):
        part = slice(h * HEAD, (h + 1) * HEAD)
        nk_ref[:, part] = (ks_ref[:, part] + a * grad_ref[:, 2 * h * HEAD : (2 * h + 1) * HEAD]) * factor
        nv_ref[:, part] = (vs_ref[:, part] + a * grad_ref[:, (2 * h + 1) * HEAD : (2 * h + 2) * HEAD]) * factor


def update(count, everything, near, ks, vs, grad):
    return pl.pallas_call(
        functools.partial(update_kernel, count),
        out_shape=[jax.ShapeDtypeStruct(ks.shape, F32)] * 2,
        compiler_params=pltpu.CompilerParams(vmem_limit_bytes=4 << 20),
        cost_estimate=pl.CostEstimate(flops=1 << 17, bytes_accessed=1 << 20, transcendentals=256),
    )(everything, near, ks, vs, grad)


def along_z(x, d):
    n = lax.axis_size("cz")
    return lax.ppermute(x, "cz", [(i - d, i) for i in range(n) if 0 <= i - d < n])


def swap_x(x):
    return lax.all_to_all(x, "cx", 0, 0)


def sum_among(x, axes):
    n = math.prod(lax.axis_size(a) for a in axes)
    return lax.all_to_all(jnp.broadcast_to(x[None], (n,) + x.shape), axes, 0, 0)


def per_device(query, key, value, key_shift, value_shift, doc_ids, target):
    tokens = query.shape[1]
    kv_local = key.shape[2] // HEAD
    where_x = lax.axis_index("cx")
    n_x = lax.axis_size("cx")
    at_x = where_x.astype(jnp.int32)[None]
    row = prepare(key[0], value[0], key_shift[0], value_shift[0], doc_ids)
    one, two = along_z(row, 1), along_z(row, 2)
    wins = []
    for h in range(kv_local):
        part = slice(2 * h * HEAD, 2 * (h + 1) * HEAD)
        near = jnp.concatenate([one[:, part], two[:, part]], 0)
        far = along_z(near, 2)
        wins.append(swap_x(spread(at_x, row, near, far, h, n_x)))
    attn = query[0]
    kept = []
    for h in range(kv_local):
        attn, gwin, gown = attention(query[0], target[0], wins[h], row, attn, h)
        sent, mine = fold(at_x, swap_x(gwin), gown)
        kept.append((along_z(sent, -2), mine))
    near = [
        jnp.concatenate(
            [
                (mine[(b + 1) * tokens : (b + 2) * tokens] + far[b * tokens : (b + 1) * tokens]).astype(BF)
                for far, mine in kept
            ],
            1,
        )
        for b in range(2)
    ]
    two, one = along_z(near[1], -2), along_z(near[0], -1)
    grad = jnp.concatenate([mine[:tokens] for _, mine in kept], 1) + one.astype(F32) + two.astype(F32)
    grad_key = jnp.concatenate(
        [grad[:, 2 * h * HEAD : (2 * h + 1) * HEAD] for h in range(kv_local)], 1
    )
    grad_val = jnp.concatenate(
        [grad[:, (2 * h + 1) * HEAD : (2 * h + 2) * HEAD] for h in range(kv_local)], 1
    )
    ks, vs = key_shift[0], value_shift[0]
    sums = jnp.stack(
        [
            jnp.sum(ks * ks, -1) + jnp.sum(vs * vs, -1),
            jnp.sum(ks * grad_key, -1) + jnp.sum(vs * grad_val, -1),
            jnp.sum(grad_key * grad_key, -1) + jnp.sum(grad_val * grad_val, -1),
        ]
    )
    n_dp, n_tp = lax.axis_size("dp"), lax.axis_size("tp")
    plane = sum_among(sums, ("dp", "cx", "tp"))
    first = ((lax.axis_index("dp") * n_x + where_x) * n_tp).astype(jnp.int32)[None]
    near, square = gather(first, plane, lax.axis_size("cz"), n_tp)
    everything = lax.all_to_all(square, "cz", 0, 0)
    count = n_dp * tokens * n_x * lax.axis_size("cz") * 2 * KV_HEADS * HEAD
    new_ks, new_vs = update(count, everything, near, ks, vs, grad)
    return attn[None], new_ks[None], new_vs[None]


def solution(mesh):
    sizes = mesh.devices.shape
    inner = Mesh(
        mesh.devices.reshape(sizes[0], sizes[1] // 4, 4, sizes[2]), ("dp", "cz", "cx", "tp")
    )
    whole = P("dp", ("cz", "cx"), "tp")
    in_specs = (whole,) * 5 + (P("dp", ("cz", "cx")), whole)
    return jax.shard_map(
        per_device, mesh=inner, in_specs=in_specs, out_specs=(whole,) * 3, check_vma=False
    )
```

```python
import functools
import math

import jax
import jax.numpy as jnp
from jax import lax
from jax.experimental import pallas as pl
from jax.experimental.pallas import tpu as pltpu
from jax.sharding import Mesh
from jax.sharding import PartitionSpec as P

HEADS = 64
KV_HEADS = 8
HEAD = 128
GROUP = HEADS // KV_HEADS
DOC_MAX = 2048

step_size = 0.1
radius_scale = 0.13

BF = jnp.bfloat16
F32 = jnp.float32
NT = (((1,), (1,)), ((), ()))
NN = (((1,), (0,)), ((), ()))
FAR = -1e30
ROWS = 4
TAIL = 8


def mm(a, b, dims=NN):
    return lax.dot_general(a, b, dims, preferred_element_type=F32)


def attn_kernel(
    q_ref, t_ref, win_ref, own_ref, _, o_ref, gwin_ref, gown_ref,
    kaug, vaug, vat, qaug, taug, s_ref, p_ref,
):
    tokens = q_ref.shape[0]
    rows_all = GROUP * tokens
    blocks = []
    for x in range(win_ref.shape[0]):
        for b in range(ROWS):
            blocks.append((win_ref.at[x], gwin_ref.at[x], b))
    blocks.append((own_ref, gown_ref, 0))
    step = tokens + TAIL
    docs = jnp.concatenate(
        [src[b * step + tokens : b * step + tokens + 1, 0:tokens].astype(F32) for src, _, b in blocks], 0
    )
    docs_sq = jnp.concatenate([docs, jnp.zeros((tokens - docs.shape[0], tokens), F32)], 0)
    doc_cols = docs_sq.T
    doc_row = docs[len(blocks) - 1 :, :]
    i_key = lax.broadcasted_iota(jnp.int32, (tokens, tokens), 0)
    i_qry = lax.broadcasted_iota(jnp.int32, (tokens, tokens), 1)
    one = jnp.ones((tokens, HEAD), BF)
    for j, (src, _, b) in enumerate(blocks):
        rows = slice(j * tokens, (j + 1) * tokens)
        kaug[rows, 0:HEAD] = src[b * step : b * step + tokens, 0:HEAD]
        v = src[b * step : b * step + tokens, HEAD : 2 * HEAD]
        vaug[rows, 0:HEAD] = v
        vaug[rows, HEAD : 2 * HEAD] = one
        vat[0:HEAD, rows] = v.T
        vat[HEAD : 2 * HEAD, rows] = one
        ok = doc_cols[:, j : j + 1] == doc_row
        if j == len(blocks) - 1:
            ok = ok & (i_key <= i_qry)
        kaug[rows, HEAD : HEAD + tokens] = jnp.where(ok, 0.0, FAR).astype(BF)
    eye = (i_key == i_qry).astype(F32).astype(BF)
    for h in range(GROUP):
        qaug[h * tokens : (h + 1) * tokens, 0:HEAD] = q_ref[:, h * HEAD : (h + 1) * HEAD]
        qaug[h * tokens : (h + 1) * tokens, HEAD : HEAD + tokens] = eye
    scores = mm(kaug[...], qaug[...], NT)
    s_ref[...] = scores
    top = jnp.max(scores.reshape(scores.shape[0] // 8, 8, rows_all), 0)
    top = jnp.max(top, 0, keepdims=True)
    c = math.log2(math.e) / math.sqrt(HEAD)
    for j in range(len(blocks)):
        rows = slice(j * tokens, (j + 1) * tokens)
        p_ref[rows, :] = jnp.exp2((s_ref[rows, :] - top) * c).astype(BF)
    lane = lax.broadcasted_iota(jnp.int32, (tokens, HEAD), 1)
    for pair in range(GROUP // 2):
        ot = mm(vat[...], p_ref[:, pair * 2 * tokens : (pair + 1) * 2 * tokens])
        for u in range(2):
            h = 2 * pair + u
            o = ot[:, u * tokens : (u + 1) * tokens].T
            inv = 1.0 / o[:, HEAD:]
            out = o[:, :HEAD] * inv
            o_ref[:, h * HEAD : (h + 1) * HEAD] = out.astype(BF)
            tp = (t_ref[:, h * HEAD : (h + 1) * HEAD].astype(F32) * inv).astype(BF)
            delta = jnp.sum(tp.astype(F32) * out, 1, keepdims=True)
            hi = delta.astype(BF).astype(F32)
            rest = delta - hi
            mid = rest.astype(BF).astype(F32)
            lo = rest - mid
            ext = jnp.where(
                lane == 0, -hi, jnp.where(lane == 1, -mid, jnp.where(lane == 2, -lo, 0.0))
            )
            taug[h * tokens : (h + 1) * tokens, 0:HEAD] = tp
            taug[h * tokens : (h + 1) * tokens, HEAD : 2 * HEAD] = ext.astype(BF)
    scale = 1.0 / math.sqrt(HEAD)
    ds = (p_ref[...].astype(F32) * mm(vaug[...], taug[...], NT)).astype(BF)
    dk = mm(ds, qaug[:, 0:HEAD]) * scale
    dv = mm(p_ref[...], taug[:, 0:HEAD])
    for j, (_, g, b) in enumerate(blocks):
        rows = slice(j * tokens, (j + 1) * tokens)
        out_rows = slice(b * tokens, (b + 1) * tokens)
        g[out_rows, 0:HEAD] = dk[rows].astype(g.dtype)
        g[out_rows, HEAD : 2 * HEAD] = dv[rows].astype(g.dtype)


def attention(q, t, win, own, attn, head):
    tokens = q.shape[0]
    n = win.shape[0]
    keys = (ROWS * n + 1) * tokens
    rows_all = GROUP * tokens
    wide = pl.BlockSpec((tokens, rows_all), lambda g: (0, head))
    whole = pl.BlockSpec(memory_space=pltpu.VMEM)
    return pl.pallas_call(
        attn_kernel,
        grid=(1,),
        in_specs=[
            wide,
            wide,
            whole,
            pl.BlockSpec((own.shape[0], 2 * HEAD), lambda g: (0, head)),
            pl.BlockSpec(memory_space=pl.ANY),
        ],
        out_specs=[wide, whole, whole],
        out_shape=[
            jax.ShapeDtypeStruct(q.shape, BF),
            jax.ShapeDtypeStruct((n, ROWS * tokens, 2 * HEAD), BF),
            jax.ShapeDtypeStruct((tokens, 2 * HEAD), F32),
        ],
        input_output_aliases={4: 0} if head else {},
        scratch_shapes=[
            pltpu.VMEM((keys, 2 * HEAD), BF),
            pltpu.VMEM((keys, 2 * HEAD), BF),
            pltpu.VMEM((2 * HEAD, keys), BF),
            pltpu.VMEM((rows_all, 2 * HEAD), BF),
            pltpu.VMEM((rows_all, 2 * HEAD), BF),
            pltpu.VMEM((keys, rows_all), F32),
            pltpu.VMEM((keys, rows_all), BF),
        ],
        compiler_params=pltpu.CompilerParams(vmem_limit_bytes=32 << 20),
        cost_estimate=pl.CostEstimate(
            flops=keys * rows_all * HEAD * 10,
            bytes_accessed=4 << 20,
            transcendentals=keys * rows_all,
        ),
    )(
        pltpu.with_memory_space_constraint(q, pltpu.HBM),
        pltpu.with_memory_space_constraint(t, pltpu.HBM),
        win,
        own,
        attn,
    )


def prepare_kernel(k_ref, v_ref, ks_ref, vs_ref, docs_ref, row_ref, first_ref):
    tokens = k_ref.shape[0]
    k = (k_ref[...].astype(F32) + ks_ref[...]).astype(BF)
    v = (v_ref[...].astype(F32) + vs_ref[...]).astype(BF)
    docs = (docs_ref[...] + 1).astype(F32)
    docs = jnp.broadcast_to(docs, (TAIL, docs.shape[1])).astype(BF)
    for h in range(k.shape[1] // HEAD):
        at = 2 * h * HEAD
        row_ref[0:tokens, at : at + HEAD] = k[:, h * HEAD : (h + 1) * HEAD]
        row_ref[0:tokens, at + HEAD : at + 2 * HEAD] = v[:, h * HEAD : (h + 1) * HEAD]
        row_ref[tokens:, at : at + tokens] = docs
        row_ref[tokens:, at + HEAD : at + HEAD + tokens] = docs
    first_ref[...] = row_ref[:, 0 : 2 * HEAD]


def prepare(k, v, ks, vs, docs):
    tokens, width = k.shape
    hbm = [pltpu.with_memory_space_constraint(x, pltpu.HBM) for x in (k, v, ks, vs, docs)]
    return pl.pallas_call(
        prepare_kernel,
        out_shape=[
            jax.ShapeDtypeStruct((tokens + TAIL, 2 * width), BF),
            jax.ShapeDtypeStruct((tokens + TAIL, 2 * HEAD), BF),
        ],
        compiler_params=pltpu.CompilerParams(vmem_limit_bytes=4 << 20),
        cost_estimate=pl.CostEstimate(flops=1 << 17, bytes_accessed=1 << 19, transcendentals=0),
    )(*hbm)


def spread_kernel(x_ref, row_ref, one_ref, two_ref, three_ref, four_ref, out_ref):
    rows = row_ref.shape[0]
    for i in range(out_ref.shape[0]):
        @pl.when(i > x_ref[0])
        def _():
            out_ref[i, 0:rows, :] = row_ref[...]

        @pl.when(i <= x_ref[0])
        def _():
            out_ref[i, 0:rows, :] = four_ref[...]

        out_ref[i, rows : 2 * rows, :] = one_ref[...]
        out_ref[i, 2 * rows : 3 * rows, :] = two_ref[...]
        out_ref[i, 3 * rows :, :] = three_ref[...]


def spread(where_x, row, one, two, three, four, head, n):
    rows, width = row.shape[0], 2 * HEAD
    at_head = pl.BlockSpec((rows, width), lambda g: (0, head))
    below = 0 if four.shape[0] == rows else 1
    return pl.pallas_call(
        spread_kernel,
        grid=(1,),
        in_specs=[
            pl.BlockSpec(memory_space=pltpu.SMEM),
            at_head,
            at_head,
            at_head,
            pl.BlockSpec((rows, width), lambda g: (0, 0)),
            pl.BlockSpec((rows, width), lambda g: (below, 0)),
        ],
        out_specs=pl.BlockSpec(memory_space=pltpu.VMEM),
        out_shape=jax.ShapeDtypeStruct((n, ROWS * rows, width), BF),
        compiler_params=pltpu.CompilerParams(vmem_limit_bytes=8 << 20),
        cost_estimate=pl.CostEstimate(flops=0, bytes_accessed=2 << 20, transcendentals=0),
    )(where_x, row, one, two, three, four)


def fold_kernel(x_ref, back_ref, gown_ref, sent_ref, kept_ref):
    tokens = gown_ref.shape[0]
    n = back_ref.shape[0]

    def part(i, b):
        return back_ref[i, b * tokens : (b + 1) * tokens, :].astype(F32)

    own = gown_ref[...]
    last = jnp.zeros_like(own)
    for i in range(n):
        later = i > x_ref[0]
        p = part(i, 0)
        own = own + jnp.where(later, p, 0.0)
        last = last + jnp.where(later, 0.0, p)
    kept_ref[0:tokens, :] = own
    for b in (1, 2):
        kept_ref[b * tokens : (b + 1) * tokens, :] = sum(part(i, b) for i in range(n))
    sent_ref[0:tokens, :] = sum(part(i, 3) for i in range(n)).astype(BF)
    sent_ref[tokens:, :] = last.astype(BF)


def fold(where_x, back, gown):
    tokens, width = gown.shape
    vmem = pl.BlockSpec(memory_space=pltpu.VMEM)
    return pl.pallas_call(
        fold_kernel,
        in_specs=[pl.BlockSpec(memory_space=pltpu.SMEM), vmem, vmem],
        out_specs=[vmem, vmem],
        out_shape=[
            jax.ShapeDtypeStruct((2 * tokens, width), BF),
            jax.ShapeDtypeStruct((3 * tokens, width), F32),
        ],
        compiler_params=pltpu.CompilerParams(vmem_limit_bytes=8 << 20),
        cost_estimate=pl.CostEstimate(flops=1 << 19, bytes_accessed=2 << 20, transcendentals=0),
    )(where_x, back, gown)


def gather_kernel(n_tp, first_ref, plane_ref, near_ref, out_ref):
    square = jnp.sum(plane_ref[:, 2, :])
    out_ref[...] = jnp.full(out_ref.shape, square, F32)
    near_ref[...] = jnp.sum(plane_ref[pl.ds(first_ref[0], n_tp)], 0)


def gather(first, plane, n, n_tp):
    vmem = pl.BlockSpec(memory_space=pltpu.VMEM)
    return pl.pallas_call(
        functools.partial(gather_kernel, n_tp),
        in_specs=[pl.BlockSpec(memory_space=pltpu.SMEM), vmem],
        out_specs=[vmem, vmem],
        out_shape=[
            jax.ShapeDtypeStruct(plane.shape[1:], F32),
            jax.ShapeDtypeStruct((n, 1, plane.shape[2]), F32),
        ],
        compiler_params=pltpu.CompilerParams(vmem_limit_bytes=4 << 20),
        cost_estimate=pl.CostEstimate(flops=1 << 14, bytes_accessed=1 << 16, transcendentals=0),
    )(first, plane)


def update_kernel(count, all_ref, near_ref, ks_ref, vs_ref, grad_ref, nk_ref, nv_ref):
    tokens = ks_ref.shape[0]
    overall = jnp.sum(all_ref[...], 0)
    a = step_size / jnp.sqrt(overall / count + 1e-05)
    near = near_ref[...]
    size_sq = jnp.maximum(near[0:1] + 2.0 * a * near[1:2] + a * a * near[2:3], 0.0)
    radius = radius_scale * math.sqrt(2 * KV_HEADS * HEAD)
    factor = jnp.minimum(1.0, radius / jnp.sqrt(size_sq + 1e-06))
    factor = jnp.broadcast_to(factor, (tokens, tokens)).T
    for h in range(ks_ref.shape[1] // HEAD):
        part = slice(h * HEAD, (h + 1) * HEAD)
        nk_ref[:, part] = (ks_ref[:, part] + a * grad_ref[:, 2 * h * HEAD : (2 * h + 1) * HEAD]) * factor
        nv_ref[:, part] = (vs_ref[:, part] + a * grad_ref[:, (2 * h + 1) * HEAD : (2 * h + 2) * HEAD]) * factor


def update(count, everything, near, ks, vs, grad):
    return pl.pallas_call(
        functools.partial(update_kernel, count),
        out_shape=[jax.ShapeDtypeStruct(ks.shape, F32)] * 2,
        compiler_params=pltpu.CompilerParams(vmem_limit_bytes=4 << 20),
        cost_estimate=pl.CostEstimate(flops=1 << 17, bytes_accessed=1 << 20, transcendentals=256),
    )(everything, near, ks, vs, grad)


def along_z(x, d):
    n = lax.axis_size("cz")
    return lax.ppermute(x, "cz", [(i - d, i) for i in range(n) if 0 <= i - d < n])


def swap_x(x):
    return lax.all_to_all(x, "cx", 0, 0)


def sum_among(x, axes):
    n = math.prod(lax.axis_size(a) for a in axes)
    return lax.all_to_all(jnp.broadcast_to(x[None], (n,) + x.shape), axes, 0, 0)


def per_device(query, key, value, key_shift, value_shift, doc_ids, target):
    tokens = query.shape[1]
    kv_local = key.shape[2] // HEAD
    where_x = lax.axis_index("cx")
    n_x = lax.axis_size("cx")
    at_x = where_x.astype(jnp.int32)[None]
    row, row_first = prepare(key[0], value[0], key_shift[0], value_shift[0], doc_ids)
    one, two = along_z(row, 1), along_z(row, 2)
    wins = []
    for h in range(kv_local):
        if h == 0:
            three, four = along_z(row_first, 3), along_z(row_first, 4)
        else:
            part = slice(2 * h * HEAD, 2 * (h + 1) * HEAD)
            three = four = along_z(jnp.concatenate([one[:, part], two[:, part]], 0), 2)
        wins.append(swap_x(spread(at_x, row, one, two, three, four, h, n_x)))
    attn = query[0]
    kept = []
    for h in range(kv_local):
        attn, gwin, gown = attention(query[0], target[0], wins[h], row, attn, h)
        sent, mine = fold(at_x, swap_x(gwin), gown)
        kept.append((along_z(sent, -2), mine))
    near = [
        jnp.concatenate(
            [
                (mine[(b + 1) * tokens : (b + 2) * tokens] + far[b * tokens : (b + 1) * tokens]).astype(BF)
                for far, mine in kept
            ],
            1,
        )
        for b in range(2)
    ]
    two, one = along_z(near[1], -2), along_z(near[0], -1)
    grad = jnp.concatenate([mine[:tokens] for _, mine in kept], 1) + one.astype(F32) + two.astype(F32)
    grad_key = jnp.concatenate(
        [grad[:, 2 * h * HEAD : (2 * h + 1) * HEAD] for h in range(kv_local)], 1
    )
    grad_val = jnp.concatenate(
        [grad[:, (2 * h + 1) * HEAD : (2 * h + 2) * HEAD] for h in range(kv_local)], 1
    )
    ks, vs = key_shift[0], value_shift[0]
    sums = jnp.stack(
        [
            jnp.sum(ks * ks, -1) + jnp.sum(vs * vs, -1),
            jnp.sum(ks * grad_key, -1) + jnp.sum(vs * grad_val, -1),
            jnp.sum(grad_key * grad_key, -1) + jnp.sum(grad_val * grad_val, -1),
        ]
    )
    n_dp, n_tp = lax.axis_size("dp"), lax.axis_size("tp")
    plane = sum_among(sums, ("dp", "cx", "tp"))
    first = ((lax.axis_index("dp") * n_x + where_x) * n_tp).astype(jnp.int32)[None]
    near, square = gather(first, plane, lax.axis_size("cz"), n_tp)
    everything = lax.all_to_all(square, "cz", 0, 0)
    count = n_dp * tokens * n_x * lax.axis_size("cz") * 2 * KV_HEADS * HEAD
    new_ks, new_vs = update(count, everything, near, ks, vs, grad)
    return attn[None], new_ks[None], new_vs[None]


def solution(mesh):
    sizes = mesh.devices.shape
    inner = Mesh(
        mesh.devices.reshape(sizes[0], sizes[1] // 4, 4, sizes[2]), ("dp", "cz", "cx", "tp")
    )
    whole = P("dp", ("cz", "cx"), "tp")
    in_specs = (whole,) * 5 + (P("dp", ("cz", "cx")), whole)
    return jax.shard_map(
        per_device, mesh=inner, in_specs=in_specs, out_specs=(whole,) * 3, check_vma=False
    )
```

```python
import functools
import math

import jax
import jax.numpy as jnp
from jax import lax
from jax.experimental import pallas as pl
from jax.experimental.pallas import tpu as pltpu
from jax.sharding import Mesh
from jax.sharding import PartitionSpec as P

HEADS = 64
KV_HEADS = 8
HEAD = 128
GROUP = HEADS // KV_HEADS
DOC_MAX = 2048

step_size = 0.1
radius_scale = 0.13

BF = jnp.bfloat16
F32 = jnp.float32
NT = (((1,), (1,)), ((), ()))
NN = (((1,), (0,)), ((), ()))
FAR = -1e30
ROWS = 4
TAIL = 8


def mm(a, b, dims=NN):
    return lax.dot_general(a, b, dims, preferred_element_type=F32)


def attn_kernel(
    q_ref, t_ref, win_ref, own_ref, _, o_ref, gwin_ref, gown_ref,
    kaug, vaug, vat, qaug, taug, s_ref, p_ref,
):
    tokens = q_ref.shape[0]
    rows_all = GROUP * tokens
    blocks = []
    for x in range(win_ref.shape[0]):
        for b in range(ROWS):
            blocks.append((win_ref.at[x], gwin_ref.at[x], b))
    blocks.append((own_ref, gown_ref, 0))
    step = tokens + TAIL
    docs = jnp.concatenate(
        [src[b * step + tokens : b * step + tokens + 1, 0:tokens].astype(F32) for src, _, b in blocks], 0
    )
    docs_sq = jnp.concatenate([docs, jnp.zeros((tokens - docs.shape[0], tokens), F32)], 0)
    doc_cols = docs_sq.T
    doc_row = docs[len(blocks) - 1 :, :]
    i_key = lax.broadcasted_iota(jnp.int32, (tokens, tokens), 0)
    i_qry = lax.broadcasted_iota(jnp.int32, (tokens, tokens), 1)
    one = jnp.ones((tokens, HEAD), BF)
    for j, (src, _, b) in enumerate(blocks):
        rows = slice(j * tokens, (j + 1) * tokens)
        kaug[rows, 0:HEAD] = src[b * step : b * step + tokens, 0:HEAD]
        v = src[b * step : b * step + tokens, HEAD : 2 * HEAD]
        vaug[rows, 0:HEAD] = v
        vaug[rows, HEAD : 2 * HEAD] = one
        vat[0:HEAD, rows] = v.T
        vat[HEAD : 2 * HEAD, rows] = one
        ok = doc_cols[:, j : j + 1] == doc_row
        if j == len(blocks) - 1:
            ok = ok & (i_key <= i_qry)
        kaug[rows, HEAD : HEAD + tokens] = jnp.where(ok, 0.0, FAR).astype(BF)
    eye = (i_key == i_qry).astype(F32).astype(BF)
    for h in range(GROUP):
        qaug[h * tokens : (h + 1) * tokens, 0:HEAD] = q_ref[:, h * HEAD : (h + 1) * HEAD]
        qaug[h * tokens : (h + 1) * tokens, HEAD : HEAD + tokens] = eye
    scores = mm(kaug[...], qaug[...], NT)
    s_ref[...] = scores
    top = jnp.max(scores.reshape(scores.shape[0] // 8, 8, rows_all), 0)
    top = jnp.max(top, 0, keepdims=True)
    c = math.log2(math.e) / math.sqrt(HEAD)
    for j in range(len(blocks)):
        rows = slice(j * tokens, (j + 1) * tokens)
        p_ref[rows, :] = jnp.exp2((s_ref[rows, :] - top) * c).astype(BF)
    lane = lax.broadcasted_iota(jnp.int32, (tokens, HEAD), 1)
    for pair in range(GROUP // 2):
        ot = mm(vat[...], p_ref[:, pair * 2 * tokens : (pair + 1) * 2 * tokens])
        for u in range(2):
            h = 2 * pair + u
            o = ot[:, u * tokens : (u + 1) * tokens].T
            inv = 1.0 / o[:, HEAD:]
            out = o[:, :HEAD] * inv
            o_ref[:, h * HEAD : (h + 1) * HEAD] = out.astype(BF)
            tp = (t_ref[:, h * HEAD : (h + 1) * HEAD].astype(F32) * inv).astype(BF)
            delta = jnp.sum(tp.astype(F32) * out, 1, keepdims=True)
            hi = delta.astype(BF).astype(F32)
            rest = delta - hi
            mid = rest.astype(BF).astype(F32)
            lo = rest - mid
            ext = jnp.where(
                lane == 0, -hi, jnp.where(lane == 1, -mid, jnp.where(lane == 2, -lo, 0.0))
            )
            taug[h * tokens : (h + 1) * tokens, 0:HEAD] = tp
            taug[h * tokens : (h + 1) * tokens, HEAD : 2 * HEAD] = ext.astype(BF)
    scale = 1.0 / math.sqrt(HEAD)
    ds = (p_ref[...].astype(F32) * mm(vaug[...], taug[...], NT)).astype(BF)
    dk = mm(ds, qaug[:, 0:HEAD]) * scale
    dv = mm(p_ref[...], taug[:, 0:HEAD])
    for j, (_, g, b) in enumerate(blocks):
        rows = slice(j * tokens, (j + 1) * tokens)
        out_rows = slice(b * tokens, (b + 1) * tokens)
        g[out_rows, 0:HEAD] = dk[rows].astype(g.dtype)
        g[out_rows, HEAD : 2 * HEAD] = dv[rows].astype(g.dtype)


def attention(q, t, win, own, attn, head):
    tokens = q.shape[0]
    n = win.shape[0]
    keys = (ROWS * n + 1) * tokens
    rows_all = GROUP * tokens
    wide = pl.BlockSpec((tokens, rows_all), lambda g: (0, head))
    whole = pl.BlockSpec(memory_space=pltpu.VMEM)
    return pl.pallas_call(
        attn_kernel,
        grid=(1,),
        in_specs=[
            wide,
            wide,
            whole,
            pl.BlockSpec((own.shape[0], 2 * HEAD), lambda g: (0, head)),
            pl.BlockSpec(memory_space=pl.ANY),
        ],
        out_specs=[wide, whole, whole],
        out_shape=[
            jax.ShapeDtypeStruct(q.shape, BF),
            jax.ShapeDtypeStruct((n, ROWS * tokens, 2 * HEAD), BF),
            jax.ShapeDtypeStruct((tokens, 2 * HEAD), F32),
        ],
        input_output_aliases={4: 0} if head else {},
        scratch_shapes=[
            pltpu.VMEM((keys, 2 * HEAD), BF),
            pltpu.VMEM((keys, 2 * HEAD), BF),
            pltpu.VMEM((2 * HEAD, keys), BF),
            pltpu.VMEM((rows_all, 2 * HEAD), BF),
            pltpu.VMEM((rows_all, 2 * HEAD), BF),
            pltpu.VMEM((keys, rows_all), F32),
            pltpu.VMEM((keys, rows_all), BF),
        ],
        compiler_params=pltpu.CompilerParams(vmem_limit_bytes=32 << 20),
        cost_estimate=pl.CostEstimate(
            flops=keys * rows_all * HEAD * 10,
            bytes_accessed=4 << 20,
            transcendentals=keys * rows_all,
        ),
    )(
        pltpu.with_memory_space_constraint(q, pltpu.HBM),
        pltpu.with_memory_space_constraint(t, pltpu.HBM),
        win,
        own,
        attn,
    )


def prepare_kernel(k_ref, v_ref, ks_ref, vs_ref, docs_ref, row_ref, first_ref):
    tokens = k_ref.shape[0]
    k = (k_ref[...].astype(F32) + ks_ref[...]).astype(BF)
    v = (v_ref[...].astype(F32) + vs_ref[...]).astype(BF)
    docs = (docs_ref[...] + 1).astype(F32)
    docs = jnp.broadcast_to(docs, (TAIL, docs.shape[1])).astype(BF)
    for h in range(k.shape[1] // HEAD):
        at = 2 * h * HEAD
        row_ref[0:tokens, at : at + HEAD] = k[:, h * HEAD : (h + 1) * HEAD]
        row_ref[0:tokens, at + HEAD : at + 2 * HEAD] = v[:, h * HEAD : (h + 1) * HEAD]
        row_ref[tokens:, at : at + tokens] = docs
        row_ref[tokens:, at + HEAD : at + HEAD + tokens] = docs
    first_ref[...] = row_ref[:, 0 : 2 * HEAD]


def prepare(k, v, ks, vs, docs):
    tokens, width = k.shape
    hbm = [pltpu.with_memory_space_constraint(x, pltpu.HBM) for x in (k, v, ks, vs, docs)]
    return pl.pallas_call(
        prepare_kernel,
        out_shape=[
            jax.ShapeDtypeStruct((tokens + TAIL, 2 * width), BF),
            jax.ShapeDtypeStruct((tokens + TAIL, 2 * HEAD), BF),
        ],
        compiler_params=pltpu.CompilerParams(vmem_limit_bytes=4 << 20),
        cost_estimate=pl.CostEstimate(flops=1 << 17, bytes_accessed=1 << 19, transcendentals=0),
    )(*hbm)


def spread_kernel(x_ref, row_ref, one_ref, two_ref, three_ref, four_ref, out_ref):
    rows = row_ref.shape[0]
    for i in range(out_ref.shape[0]):
        @pl.when(i > x_ref[0])
        def _():
            out_ref[i, 0:rows, :] = row_ref[...]

        @pl.when(i <= x_ref[0])
        def _():
            out_ref[i, 0:rows, :] = four_ref[...]

        out_ref[i, rows : 2 * rows, :] = one_ref[...]
        out_ref[i, 2 * rows : 3 * rows, :] = two_ref[...]
        out_ref[i, 3 * rows :, :] = three_ref[...]


def spread(where_x, row, one, two, three, four, head, n):
    rows, width = row.shape[0], 2 * HEAD
    at_head = pl.BlockSpec((rows, width), lambda g: (0, head))
    below = 0 if four.shape[0] == rows else 1
    return pl.pallas_call(
        spread_kernel,
        grid=(1,),
        in_specs=[
            pl.BlockSpec(memory_space=pltpu.SMEM),
            at_head,
            at_head,
            at_head,
            pl.BlockSpec((rows, width), lambda g: (0, 0)),
            pl.BlockSpec((rows, width), lambda g: (below, 0)),
        ],
        out_specs=pl.BlockSpec(memory_space=pltpu.VMEM),
        out_shape=jax.ShapeDtypeStruct((n, ROWS * rows, width), BF),
        compiler_params=pltpu.CompilerParams(vmem_limit_bytes=8 << 20),
        cost_estimate=pl.CostEstimate(flops=0, bytes_accessed=2 << 20, transcendentals=0),
    )(where_x, row, one, two, three, four)


def fold_kernel(x_ref, back_ref, gown_ref, kept_ref, *sent_refs):
    tokens = gown_ref.shape[0]
    n = back_ref.shape[0]

    def part(i, b):
        return back_ref[i, b * tokens : (b + 1) * tokens, :].astype(F32)

    own = gown_ref[...]
    last = jnp.zeros_like(own)
    for i in range(n):
        later = i > x_ref[0]
        p = part(i, 0)
        own = own + jnp.where(later, p, 0.0)
        last = last + jnp.where(later, 0.0, p)
    kept_ref[0:tokens, :] = own
    for b in (1, 2):
        kept_ref[b * tokens : (b + 1) * tokens, :] = sum(part(i, b) for i in range(n))
    sent_refs[0][0:tokens, :] = sum(part(i, 3) for i in range(n)).astype(BF)
    sent_refs[-1][(2 - len(sent_refs)) * tokens :, :] = last.astype(BF)


def fold(where_x, back, gown, apart):
    tokens, width = gown.shape
    vmem = pl.BlockSpec(memory_space=pltpu.VMEM)
    return pl.pallas_call(
        fold_kernel,
        in_specs=[pl.BlockSpec(memory_space=pltpu.SMEM), vmem, vmem],
        out_specs=[vmem] * (3 if apart else 2),
        out_shape=[jax.ShapeDtypeStruct((3 * tokens, width), F32)]
        + [jax.ShapeDtypeStruct((tokens if apart else 2 * tokens, width), BF)] * (2 if apart else 1),
        compiler_params=pltpu.CompilerParams(vmem_limit_bytes=8 << 20),
        cost_estimate=pl.CostEstimate(flops=1 << 19, bytes_accessed=2 << 20, transcendentals=0),
    )(where_x, back, gown)


def gather_kernel(n_tp, first_ref, plane_ref, near_ref, out_ref):
    square = jnp.sum(plane_ref[:, 2, :])
    out_ref[...] = jnp.full(out_ref.shape, square, F32)
    near_ref[...] = jnp.sum(plane_ref[pl.ds(first_ref[0], n_tp)], 0)


def gather(first, plane, n, n_tp):
    vmem = pl.BlockSpec(memory_space=pltpu.VMEM)
    return pl.pallas_call(
        functools.partial(gather_kernel, n_tp),
        in_specs=[pl.BlockSpec(memory_space=pltpu.SMEM), vmem],
        out_specs=[vmem, vmem],
        out_shape=[
            jax.ShapeDtypeStruct(plane.shape[1:], F32),
            jax.ShapeDtypeStruct((n, 1, plane.shape[2]), F32),
        ],
        compiler_params=pltpu.CompilerParams(vmem_limit_bytes=4 << 20),
        cost_estimate=pl.CostEstimate(flops=1 << 14, bytes_accessed=1 << 16, transcendentals=0),
    )(first, plane)


def update_kernel(count, all_ref, near_ref, ks_ref, vs_ref, grad_ref, nk_ref, nv_ref):
    tokens = ks_ref.shape[0]
    overall = jnp.sum(all_ref[...], 0)
    a = step_size / jnp.sqrt(overall / count + 1e-05)
    near = near_ref[...]
    size_sq = jnp.maximum(near[0:1] + 2.0 * a * near[1:2] + a * a * near[2:3], 0.0)
    radius = radius_scale * math.sqrt(2 * KV_HEADS * HEAD)
    factor = jnp.minimum(1.0, radius / jnp.sqrt(size_sq + 1e-06))
    factor = jnp.broadcast_to(factor, (tokens, tokens)).T
    for h in range(ks_ref.shape[1] // HEAD):
        part = slice(h * HEAD, (h + 1) * HEAD)
        nk_ref[:, part] = (ks_ref[:, part] + a * grad_ref[:, 2 * h * HEAD : (2 * h + 1) * HEAD]) * factor
        nv_ref[:, part] = (vs_ref[:, part] + a * grad_ref[:, (2 * h + 1) * HEAD : (2 * h + 2) * HEAD]) * factor


def update(count, everything, near, ks, vs, grad):
    return pl.pallas_call(
        functools.partial(update_kernel, count),
        out_shape=[jax.ShapeDtypeStruct(ks.shape, F32)] * 2,
        compiler_params=pltpu.CompilerParams(vmem_limit_bytes=4 << 20),
        cost_estimate=pl.CostEstimate(flops=1 << 17, bytes_accessed=1 << 20, transcendentals=256),
    )(everything, near, ks, vs, grad)


def along_z(x, d):
    n = lax.axis_size("cz")
    return lax.ppermute(x, "cz", [(i - d, i) for i in range(n) if 0 <= i - d < n])


def swap_x(x):
    return lax.all_to_all(x, "cx", 0, 0)


def sum_among(x, axes):
    n = math.prod(lax.axis_size(a) for a in axes)
    return lax.all_to_all(jnp.broadcast_to(x[None], (n,) + x.shape), axes, 0, 0)


def per_device(query, key, value, key_shift, value_shift, doc_ids, target):
    tokens = query.shape[1]
    kv_local = key.shape[2] // HEAD
    where_x = lax.axis_index("cx")
    n_x = lax.axis_size("cx")
    at_x = where_x.astype(jnp.int32)[None]
    row, row_first = prepare(key[0], value[0], key_shift[0], value_shift[0], doc_ids)
    one, two = along_z(row, 1), along_z(row, 2)
    wins = []
    for h in range(kv_local):
        if h == 0:
            three, four = along_z(row_first, 3), along_z(row_first, 4)
        else:
            part = slice(2 * h * HEAD, 2 * (h + 1) * HEAD)
            three = four = along_z(jnp.concatenate([one[:, part], two[:, part]], 0), 2)
        wins.append(swap_x(spread(at_x, row, one, two, three, four, h, n_x)))
    attn = query[0]
    kept, ones, twos, late = [], [], [], []
    for h in range(kv_local):
        attn, gwin, gown = attention(query[0], target[0], wins[h], row, attn, h)
        last = h == kv_local - 1
        gwin = pltpu.with_memory_space_constraint(gwin, pltpu.HBM)
        back = pltpu.with_memory_space_constraint(swap_x(gwin), pltpu.HBM)
        mine, *sent = fold(at_x, back, gown, last)
        part1, part2 = mine[tokens : 2 * tokens], mine[2 * tokens :]
        if last:
            late = [along_z(sent[0], -3), along_z(sent[1], -4)]
        else:
            far = along_z(sent[0], -2).astype(F32)
            part1, part2 = part1 + far[:tokens], part2 + far[tokens:]
        kept.append(mine[:tokens])
        ones.append(part1.astype(BF))
        twos.append(part2.astype(BF))
    two = along_z(jnp.concatenate(twos, 1), -2).astype(F32)
    one = along_z(jnp.concatenate(ones, 1), -1).astype(F32)
    kept[-1] = kept[-1] + sum(x.astype(F32) for x in late)
    grad = jnp.concatenate(kept, 1) + one + two
    grad_key = jnp.concatenate(
        [grad[:, 2 * h * HEAD : (2 * h + 1) * HEAD] for h in range(kv_local)], 1
    )
    grad_val = jnp.concatenate(
        [grad[:, (2 * h + 1) * HEAD : (2 * h + 2) * HEAD] for h in range(kv_local)], 1
    )
    ks, vs = key_shift[0], value_shift[0]
    sums = jnp.stack(
        [
            jnp.sum(ks * ks, -1) + jnp.sum(vs * vs, -1),
            jnp.sum(ks * grad_key, -1) + jnp.sum(vs * grad_val, -1),
            jnp.sum(grad_key * grad_key, -1) + jnp.sum(grad_val * grad_val, -1),
        ]
    )
    n_dp, n_tp = lax.axis_size("dp"), lax.axis_size("tp")
    plane = sum_among(sums, ("dp", "cx", "tp"))
    first = ((lax.axis_index("dp") * n_x + where_x) * n_tp).astype(jnp.int32)[None]
    near, square = gather(first, plane, lax.axis_size("cz"), n_tp)
    everything = lax.all_to_all(square, "cz", 0, 0)
    count = n_dp * tokens * n_x * lax.axis_size("cz") * 2 * KV_HEADS * HEAD
    new_ks, new_vs = update(count, everything, near, ks, vs, grad)
    return attn[None], new_ks[None], new_vs[None]


def solution(mesh):
    sizes = mesh.devices.shape
    inner = Mesh(
        mesh.devices.reshape(sizes[0], sizes[1] // 4, 4, sizes[2]), ("dp", "cz", "cx", "tp")
    )
    whole = P("dp", ("cz", "cx"), "tp")
    in_specs = (whole,) * 5 + (P("dp", ("cz", "cx")), whole)
    return jax.shard_map(
        per_device, mesh=inner, in_specs=in_specs, out_specs=(whole,) * 3, check_vma=False
    )
```

```python
import functools
import math

import jax
import jax.numpy as jnp
from jax import lax
from jax.experimental import pallas as pl
from jax.experimental.pallas import tpu as pltpu
from jax.sharding import Mesh
from jax.sharding import PartitionSpec as P

HEADS = 64
KV_HEADS = 8
HEAD = 128
GROUP = HEADS // KV_HEADS
DOC_MAX = 2048

step_size = 0.1
radius_scale = 0.13

BF = jnp.bfloat16
F32 = jnp.float32
NT = (((1,), (1,)), ((), ()))
NN = (((1,), (0,)), ((), ()))
FAR = -1e30
ROWS = 4
TAIL = 8


def mm(a, b, dims=NN):
    return lax.dot_general(a, b, dims, preferred_element_type=F32)


def attn_kernel(
    q_ref, t_ref, win_ref, own_ref, _, o_ref, gwin_ref, gown_ref,
    kaug, vaug, vat, qaug, taug, s_ref, p_ref,
):
    tokens = q_ref.shape[0]
    rows_all = GROUP * tokens
    blocks = []
    for x in range(win_ref.shape[0]):
        for b in range(ROWS):
            blocks.append((win_ref.at[x], gwin_ref.at[x], b))
    blocks.append((own_ref, gown_ref, 0))
    step = tokens + TAIL
    docs = jnp.concatenate(
        [src[b * step + tokens : b * step + tokens + 1, 0:tokens].astype(F32) for src, _, b in blocks], 0
    )
    docs_sq = jnp.concatenate([docs, jnp.zeros((tokens - docs.shape[0], tokens), F32)], 0)
    doc_cols = docs_sq.T
    doc_row = docs[len(blocks) - 1 :, :]
    i_key = lax.broadcasted_iota(jnp.int32, (tokens, tokens), 0)
    i_qry = lax.broadcasted_iota(jnp.int32, (tokens, tokens), 1)
    one = jnp.ones((tokens, HEAD), BF)
    for j, (src, _, b) in enumerate(blocks):
        rows = slice(j * tokens, (j + 1) * tokens)
        kaug[rows, 0:HEAD] = src[b * step : b * step + tokens, 0:HEAD]
        v = src[b * step : b * step + tokens, HEAD : 2 * HEAD]
        vaug[rows, 0:HEAD] = v
        vaug[rows, HEAD : 2 * HEAD] = one
        vat[0:HEAD, rows] = v.T
        vat[HEAD : 2 * HEAD, rows] = one
        ok = doc_cols[:, j : j + 1] == doc_row
        if j == len(blocks) - 1:
            ok = ok & (i_key <= i_qry)
        kaug[rows, HEAD : HEAD + tokens] = jnp.where(ok, 0.0, FAR).astype(BF)
    eye = (i_key == i_qry).astype(F32).astype(BF)
    for h in range(GROUP):
        qaug[h * tokens : (h + 1) * tokens, 0:HEAD] = q_ref[:, h * HEAD : (h + 1) * HEAD]
        qaug[h * tokens : (h + 1) * tokens, HEAD : HEAD + tokens] = eye
    scores = mm(kaug[...], qaug[...], NT)
    s_ref[...] = scores
    top = jnp.max(scores.reshape(scores.shape[0] // 8, 8, rows_all), 0)
    top = jnp.max(top, 0, keepdims=True)
    c = math.log2(math.e) / math.sqrt(HEAD)
    for j in range(len(blocks)):
        rows = slice(j * tokens, (j + 1) * tokens)
        p_ref[rows, :] = jnp.exp2((s_ref[rows, :] - top) * c).astype(BF)
    lane = lax.broadcasted_iota(jnp.int32, (tokens, HEAD), 1)
    for pair in range(GROUP // 2):
        ot = mm(vat[...], p_ref[:, pair * 2 * tokens : (pair + 1) * 2 * tokens])
        for u in range(2):
            h = 2 * pair + u
            o = ot[:, u * tokens : (u + 1) * tokens].T
            inv = 1.0 / o[:, HEAD:]
            out = o[:, :HEAD] * inv
            o_ref[:, h * HEAD : (h + 1) * HEAD] = out.astype(BF)
            tp = (t_ref[:, h * HEAD : (h + 1) * HEAD].astype(F32) * inv).astype(BF)
            delta = jnp.sum(tp.astype(F32) * out, 1, keepdims=True)
            hi = delta.astype(BF).astype(F32)
            rest = delta - hi
            mid = rest.astype(BF).astype(F32)
            lo = rest - mid
            ext = jnp.where(
                lane == 0, -hi, jnp.where(lane == 1, -mid, jnp.where(lane == 2, -lo, 0.0))
            )
            taug[h * tokens : (h + 1) * tokens, 0:HEAD] = tp
            taug[h * tokens : (h + 1) * tokens, HEAD : 2 * HEAD] = ext.astype(BF)
    scale = 1.0 / math.sqrt(HEAD)
    ds = (p_ref[...].astype(F32) * mm(vaug[...], taug[...], NT)).astype(BF)
    dk = mm(ds, qaug[:, 0:HEAD]) * scale
    dv = mm(p_ref[...], taug[:, 0:HEAD])
    for j, (_, g, b) in enumerate(blocks):
        rows = slice(j * tokens, (j + 1) * tokens)
        out_rows = slice(b * tokens, (b + 1) * tokens)
        g[out_rows, 0:HEAD] = dk[rows].astype(g.dtype)
        g[out_rows, HEAD : 2 * HEAD] = dv[rows].astype(g.dtype)


def attention(q, t, win, own, attn, head):
    tokens = q.shape[0]
    n = win.shape[0]
    keys = (ROWS * n + 1) * tokens
    rows_all = GROUP * tokens
    wide = pl.BlockSpec((tokens, rows_all), lambda g: (0, head))
    whole = pl.BlockSpec(memory_space=pltpu.VMEM)
    return pl.pallas_call(
        attn_kernel,
        grid=(1,),
        in_specs=[
            wide,
            wide,
            whole,
            pl.BlockSpec((own.shape[0], 2 * HEAD), lambda g: (0, head)),
            pl.BlockSpec(memory_space=pl.ANY),
        ],
        out_specs=[wide, whole, whole],
        out_shape=[
            jax.ShapeDtypeStruct(q.shape, BF),
            jax.ShapeDtypeStruct((n, ROWS * tokens, 2 * HEAD), BF),
            jax.ShapeDtypeStruct((tokens, 2 * HEAD), F32),
        ],
        input_output_aliases={4: 0} if head else {},
        scratch_shapes=[
            pltpu.VMEM((keys, 2 * HEAD), BF),
            pltpu.VMEM((keys, 2 * HEAD), BF),
            pltpu.VMEM((2 * HEAD, keys), BF),
            pltpu.VMEM((rows_all, 2 * HEAD), BF),
            pltpu.VMEM((rows_all, 2 * HEAD), BF),
            pltpu.VMEM((keys, rows_all), F32),
            pltpu.VMEM((keys, rows_all), BF),
        ],
        compiler_params=pltpu.CompilerParams(vmem_limit_bytes=32 << 20),
        cost_estimate=pl.CostEstimate(
            flops=keys * rows_all * HEAD * 10,
            bytes_accessed=4 << 20,
            transcendentals=keys * rows_all,
        ),
    )(
        pltpu.with_memory_space_constraint(q, pltpu.HBM),
        pltpu.with_memory_space_constraint(t, pltpu.HBM),
        win,
        own,
        attn,
    )


def prepare_kernel(k_ref, v_ref, ks_ref, vs_ref, docs_ref, row_ref, first_ref):
    tokens = k_ref.shape[0]
    k = (k_ref[...].astype(F32) + ks_ref[...]).astype(BF)
    v = (v_ref[...].astype(F32) + vs_ref[...]).astype(BF)
    docs = (docs_ref[...] + 1).astype(F32)
    docs = jnp.broadcast_to(docs, (TAIL, docs.shape[1])).astype(BF)
    for h in range(k.shape[1] // HEAD):
        at = 2 * h * HEAD
        row_ref[0:tokens, at : at + HEAD] = k[:, h * HEAD : (h + 1) * HEAD]
        row_ref[0:tokens, at + HEAD : at + 2 * HEAD] = v[:, h * HEAD : (h + 1) * HEAD]
        row_ref[tokens:, at : at + tokens] = docs
        row_ref[tokens:, at + HEAD : at + HEAD + tokens] = docs
    first_ref[...] = row_ref[:, 0 : 2 * HEAD]


def prepare(k, v, ks, vs, docs):
    tokens, width = k.shape
    hbm = [pltpu.with_memory_space_constraint(x, pltpu.HBM) for x in (k, v, ks, vs, docs)]
    return pl.pallas_call(
        prepare_kernel,
        out_shape=[
            jax.ShapeDtypeStruct((tokens + TAIL, 2 * width), BF),
            jax.ShapeDtypeStruct((tokens + TAIL, 2 * HEAD), BF),
        ],
        compiler_params=pltpu.CompilerParams(vmem_limit_bytes=4 << 20),
        cost_estimate=pl.CostEstimate(flops=1 << 17, bytes_accessed=1 << 19, transcendentals=0),
    )(*hbm)


def spread_kernel(x_ref, four_ref, three_ref, two_ref, one_ref, row_ref, out_ref):
    rows = row_ref.shape[0]
    for i in range(out_ref.shape[0]):
        @pl.when(i > x_ref[0])
        def _():
            out_ref[i, 0:rows, :] = row_ref[...]

        @pl.when(i <= x_ref[0])
        def _():
            out_ref[i, 0:rows, :] = four_ref[...]

        out_ref[i, rows : 2 * rows, :] = one_ref[...]
        out_ref[i, 2 * rows : 3 * rows, :] = two_ref[...]
        out_ref[i, 3 * rows :, :] = three_ref[...]


def spread(where_x, row, one, two, three, four, head, n):
    rows, width = row.shape[0], 2 * HEAD
    at_head = pl.BlockSpec((rows, width), lambda g: (0, head))
    below = 0 if four.shape[0] == rows else 1
    return pl.pallas_call(
        spread_kernel,
        grid=(1,),
        in_specs=[
            pl.BlockSpec(memory_space=pltpu.SMEM),
            pl.BlockSpec((rows, width), lambda g: (below, 0)),
            pl.BlockSpec((rows, width), lambda g: (0, 0)),
            at_head,
            at_head,
            at_head,
        ],
        out_specs=pl.BlockSpec(memory_space=pltpu.VMEM),
        out_shape=jax.ShapeDtypeStruct((n, ROWS * rows, width), BF),
        compiler_params=pltpu.CompilerParams(vmem_limit_bytes=8 << 20),
        cost_estimate=pl.CostEstimate(flops=0, bytes_accessed=2 << 20, transcendentals=0),
    )(where_x, four, three, two, one, row)


def fold_kernel(x_ref, back_ref, gown_ref, sent_ref, kept_ref):
    tokens = gown_ref.shape[0]
    n = back_ref.shape[0]

    def part(i, b):
        return back_ref[i, b * tokens : (b + 1) * tokens, :].astype(F32)

    own = gown_ref[...]
    last = jnp.zeros_like(own)
    for i in range(n):
        later = i > x_ref[0]
        p = part(i, 0)
        own = own + jnp.where(later, p, 0.0)
        last = last + jnp.where(later, 0.0, p)
    kept_ref[0:tokens, :] = own
    for b in (1, 2):
        kept_ref[b * tokens : (b + 1) * tokens, :] = sum(part(i, b) for i in range(n))
    sent_ref[0:tokens, :] = sum(part(i, 3) for i in range(n)).astype(BF)
    sent_ref[tokens:, :] = last.astype(BF)


def fold(where_x, back, gown):
    tokens, width = gown.shape
    vmem = pl.BlockSpec(memory_space=pltpu.VMEM)
    return pl.pallas_call(
        fold_kernel,
        in_specs=[pl.BlockSpec(memory_space=pltpu.SMEM), vmem, vmem],
        out_specs=[vmem, vmem],
        out_shape=[
            jax.ShapeDtypeStruct((2 * tokens, width), BF),
            jax.ShapeDtypeStruct((3 * tokens, width), F32),
        ],
        compiler_params=pltpu.CompilerParams(vmem_limit_bytes=8 << 20),
        cost_estimate=pl.CostEstimate(flops=1 << 19, bytes_accessed=2 << 20, transcendentals=0),
    )(where_x, back, gown)


def gather_kernel(n_tp, first_ref, plane_ref, near_ref, out_ref):
    square = jnp.sum(plane_ref[:, 2, :])
    out_ref[...] = jnp.full(out_ref.shape, square, F32)
    near_ref[...] = jnp.sum(plane_ref[pl.ds(first_ref[0], n_tp)], 0)


def gather(first, plane, n, n_tp):
    vmem = pl.BlockSpec(memory_space=pltpu.VMEM)
    return pl.pallas_call(
        functools.partial(gather_kernel, n_tp),
        in_specs=[pl.BlockSpec(memory_space=pltpu.SMEM), vmem],
        out_specs=[vmem, vmem],
        out_shape=[
            jax.ShapeDtypeStruct(plane.shape[1:], F32),
            jax.ShapeDtypeStruct((n, 1, plane.shape[2]), F32),
        ],
        compiler_params=pltpu.CompilerParams(vmem_limit_bytes=4 << 20),
        cost_estimate=pl.CostEstimate(flops=1 << 14, bytes_accessed=1 << 16, transcendentals=0),
    )(first, plane)


def update_kernel(count, all_ref, near_ref, ks_ref, vs_ref, grad_ref, nk_ref, nv_ref):
    tokens = ks_ref.shape[0]
    overall = jnp.sum(all_ref[...], 0)
    a = step_size / jnp.sqrt(overall / count + 1e-05)
    near = near_ref[...]
    size_sq = jnp.maximum(near[0:1] + 2.0 * a * near[1:2] + a * a * near[2:3], 0.0)
    radius = radius_scale * math.sqrt(2 * KV_HEADS * HEAD)
    factor = jnp.minimum(1.0, radius / jnp.sqrt(size_sq + 1e-06))
    factor = jnp.broadcast_to(factor, (tokens, tokens)).T
    for h in range(ks_ref.shape[1] // HEAD):
        part = slice(h * HEAD, (h + 1) * HEAD)
        nk_ref[:, part] = (ks_ref[:, part] + a * grad_ref[:, 2 * h * HEAD : (2 * h + 1) * HEAD]) * factor
        nv_ref[:, part] = (vs_ref[:, part] + a * grad_ref[:, (2 * h + 1) * HEAD : (2 * h + 2) * HEAD]) * factor


def update(count, everything, near, ks, vs, grad):
    return pl.pallas_call(
        functools.partial(update_kernel, count),
        out_shape=[jax.ShapeDtypeStruct(ks.shape, F32)] * 2,
        compiler_params=pltpu.CompilerParams(vmem_limit_bytes=4 << 20),
        cost_estimate=pl.CostEstimate(flops=1 << 17, bytes_accessed=1 << 20, transcendentals=256),
    )(everything, near, ks, vs, grad)


def along_z(x, d):
    n = lax.axis_size("cz")
    return lax.ppermute(x, "cz", [(i - d, i) for i in range(n) if 0 <= i - d < n])


def swap_x(x):
    return lax.all_to_all(x, "cx", 0, 0)


def sum_among(x, axes):
    n = math.prod(lax.axis_size(a) for a in axes)
    return lax.all_to_all(jnp.broadcast_to(x[None], (n,) + x.shape), axes, 0, 0)


def per_device(query, key, value, key_shift, value_shift, doc_ids, target):
    tokens = query.shape[1]
    kv_local = key.shape[2] // HEAD
    where_x = lax.axis_index("cx")
    n_x = lax.axis_size("cx")
    at_x = where_x.astype(jnp.int32)[None]
    row, row_first = prepare(key[0], value[0], key_shift[0], value_shift[0], doc_ids)
    four, three = along_z(row_first, 4), along_z(row_first, 3)
    two, one = along_z(row, 2), along_z(row, 1)
    wins = []
    for h in range(kv_local):
        if h > 0:
            part = slice(2 * h * HEAD, 2 * (h + 1) * HEAD)
            three = four = along_z(jnp.concatenate([one[:, part], two[:, part]], 0), 2)
        wins.append(swap_x(spread(at_x, row, one, two, three, four, h, n_x)))
    attn = query[0]
    kept = []
    for h in range(kv_local):
        attn, gwin, gown = attention(query[0], target[0], wins[h], row, attn, h)
        sent, mine = fold(at_x, swap_x(gwin), gown)
        kept.append((along_z(sent, -2), mine))
    near = [
        jnp.concatenate(
            [
                (mine[(b + 1) * tokens : (b + 2) * tokens] + far[b * tokens : (b + 1) * tokens]).astype(BF)
                for far, mine in kept
            ],
            1,
        )
        for b in range(2)
    ]
    two, one = along_z(near[1], -2), along_z(near[0], -1)
    grad = jnp.concatenate([mine[:tokens] for _, mine in kept], 1) + one.astype(F32) + two.astype(F32)
    grad_key = jnp.concatenate(
        [grad[:, 2 * h * HEAD : (2 * h + 1) * HEAD] for h in range(kv_local)], 1
    )
    grad_val = jnp.concatenate(
        [grad[:, (2 * h + 1) * HEAD : (2 * h + 2) * HEAD] for h in range(kv_local)], 1
    )
    ks, vs = key_shift[0], value_shift[0]
    sums = jnp.stack(
        [
            jnp.sum(ks * ks, -1) + jnp.sum(vs * vs, -1),
            jnp.sum(ks * grad_key, -1) + jnp.sum(vs * grad_val, -1),
            jnp.sum(grad_key * grad_key, -1) + jnp.sum(grad_val * grad_val, -1),
        ]
    )
    n_dp, n_tp = lax.axis_size("dp"), lax.axis_size("tp")
    first = ((lax.axis_index("dp") * n_x + where_x) * n_tp).astype(jnp.int32)[None]
    sums, first = lax.optimization_barrier((sums, first))
    plane = sum_among(sums, ("dp", "cx", "tp"))
    near, square = gather(first, plane, lax.axis_size("cz"), n_tp)
    everything = lax.all_to_all(square, "cz", 0, 0)
    count = n_dp * tokens * n_x * lax.axis_size("cz") * 2 * KV_HEADS * HEAD
    new_ks, new_vs = update(count, everything, near, ks, vs, grad)
    return attn[None], new_ks[None], new_vs[None]


def solution(mesh):
    sizes = mesh.devices.shape
    inner = Mesh(
        mesh.devices.reshape(sizes[0], sizes[1] // 4, 4, sizes[2]), ("dp", "cz", "cx", "tp")
    )
    whole = P("dp", ("cz", "cx"), "tp")
    in_specs = (whole,) * 5 + (P("dp", ("cz", "cx")), whole)
    return jax.shard_map(
        per_device, mesh=inner, in_specs=in_specs, out_specs=(whole,) * 3, check_vma=False
    )
```

```python
import functools
import math

import jax
import jax.numpy as jnp
from jax import lax
from jax.experimental import pallas as pl
from jax.experimental.pallas import tpu as pltpu
from jax.sharding import Mesh
from jax.sharding import PartitionSpec as P

HEADS = 64
KV_HEADS = 8
HEAD = 128
GROUP = HEADS // KV_HEADS
DOC_MAX = 2048

step_size = 0.1
radius_scale = 0.13

BF = jnp.bfloat16
F32 = jnp.float32
NT = (((1,), (1,)), ((), ()))
NN = (((1,), (0,)), ((), ()))
FAR = -1e30
ROWS = 4
TAIL = 8


def mm(a, b, dims=NN):
    return lax.dot_general(a, b, dims, preferred_element_type=F32)


def attn_kernel(
    q_ref, t_ref, win_ref, own_ref, _, o_ref, gwin_ref, gown_ref,
    kaug, vaug, vat, qaug, taug, s_ref, p_ref,
):
    tokens = q_ref.shape[0]
    rows_all = GROUP * tokens
    blocks = []
    for x in range(win_ref.shape[0]):
        for b in range(ROWS):
            blocks.append((win_ref.at[x], gwin_ref.at[x], b))
    blocks.append((own_ref, gown_ref, 0))
    step = tokens + TAIL
    docs = jnp.concatenate(
        [src[b * step + tokens : b * step + tokens + 1, 0:tokens].astype(F32) for src, _, b in blocks], 0
    )
    docs_sq = jnp.concatenate([docs, jnp.zeros((tokens - docs.shape[0], tokens), F32)], 0)
    doc_cols = docs_sq.T
    doc_row = docs[len(blocks) - 1 :, :]
    i_key = lax.broadcasted_iota(jnp.int32, (tokens, tokens), 0)
    i_qry = lax.broadcasted_iota(jnp.int32, (tokens, tokens), 1)
    one = jnp.ones((tokens, HEAD), BF)
    for j, (src, _, b) in enumerate(blocks):
        rows = slice(j * tokens, (j + 1) * tokens)
        kaug[rows, 0:HEAD] = src[b * step : b * step + tokens, 0:HEAD]
        v = src[b * step : b * step + tokens, HEAD : 2 * HEAD]
        vaug[rows, 0:HEAD] = v
        vaug[rows, HEAD : 2 * HEAD] = one
        vat[0:HEAD, rows] = v.T
        vat[HEAD : 2 * HEAD, rows] = one
        ok = doc_cols[:, j : j + 1] == doc_row
        if j == len(blocks) - 1:
            ok = ok & (i_key <= i_qry)
        kaug[rows, HEAD : HEAD + tokens] = jnp.where(ok, 0.0, FAR).astype(BF)
    eye = (i_key == i_qry).astype(F32).astype(BF)
    for h in range(GROUP):
        qaug[h * tokens : (h + 1) * tokens, 0:HEAD] = q_ref[:, h * HEAD : (h + 1) * HEAD]
        qaug[h * tokens : (h + 1) * tokens, HEAD : HEAD + tokens] = eye
    scores = mm(kaug[...], qaug[...], NT)
    s_ref[...] = scores
    top = jnp.max(scores.reshape(scores.shape[0] // 8, 8, rows_all), 0)
    top = jnp.max(top, 0, keepdims=True)
    c = math.log2(math.e) / math.sqrt(HEAD)
    for j in range(len(blocks)):
        rows = slice(j * tokens, (j + 1) * tokens)
        p_ref[rows, :] = jnp.exp2((s_ref[rows, :] - top) * c).astype(BF)
    lane = lax.broadcasted_iota(jnp.int32, (tokens, HEAD), 1)
    for pair in range(GROUP // 2):
        ot = mm(vat[...], p_ref[:, pair * 2 * tokens : (pair + 1) * 2 * tokens])
        for u in range(2):
            h = 2 * pair + u
            o = ot[:, u * tokens : (u + 1) * tokens].T
            inv = 1.0 / o[:, HEAD:]
            out = o[:, :HEAD] * inv
            o_ref[:, h * HEAD : (h + 1) * HEAD] = out.astype(BF)
            tp = (t_ref[:, h * HEAD : (h + 1) * HEAD].astype(F32) * inv).astype(BF)
            delta = jnp.sum(tp.astype(F32) * out, 1, keepdims=True)
            hi = delta.astype(BF).astype(F32)
            rest = delta - hi
            mid = rest.astype(BF).astype(F32)
            lo = rest - mid
            ext = jnp.where(
                lane == 0, -hi, jnp.where(lane == 1, -mid, jnp.where(lane == 2, -lo, 0.0))
            )
            taug[h * tokens : (h + 1) * tokens, 0:HEAD] = tp
            taug[h * tokens : (h + 1) * tokens, HEAD : 2 * HEAD] = ext.astype(BF)
    scale = 1.0 / math.sqrt(HEAD)
    ds = (p_ref[...].astype(F32) * mm(vaug[...], taug[...], NT)).astype(BF)
    dk = mm(ds, qaug[:, 0:HEAD]) * scale
    dv = mm(p_ref[...], taug[:, 0:HEAD])
    for j, (_, g, b) in enumerate(blocks):
        rows = slice(j * tokens, (j + 1) * tokens)
        out_rows = slice(b * tokens, (b + 1) * tokens)
        g[out_rows, 0:HEAD] = dk[rows].astype(g.dtype)
        g[out_rows, HEAD : 2 * HEAD] = dv[rows].astype(g.dtype)


def attention(q, t, win, own, attn, head):
    tokens = q.shape[0]
    n = win.shape[0]
    keys = (ROWS * n + 1) * tokens
    rows_all = GROUP * tokens
    wide = pl.BlockSpec((tokens, rows_all), lambda g: (0, head))
    whole = pl.BlockSpec(memory_space=pltpu.VMEM)
    return pl.pallas_call(
        attn_kernel,
        grid=(1,),
        in_specs=[
            wide,
            wide,
            whole,
            pl.BlockSpec((own.shape[0], 2 * HEAD), lambda g: (0, head)),
            pl.BlockSpec(memory_space=pl.ANY),
        ],
        out_specs=[wide, whole, whole],
        out_shape=[
            jax.ShapeDtypeStruct(q.shape, BF),
            jax.ShapeDtypeStruct((n, ROWS * tokens, 2 * HEAD), BF),
            jax.ShapeDtypeStruct((tokens, 2 * HEAD), F32),
        ],
        input_output_aliases={4: 0} if head else {},
        scratch_shapes=[
            pltpu.VMEM((keys, 2 * HEAD), BF),
            pltpu.VMEM((keys, 2 * HEAD), BF),
            pltpu.VMEM((2 * HEAD, keys), BF),
            pltpu.VMEM((rows_all, 2 * HEAD), BF),
            pltpu.VMEM((rows_all, 2 * HEAD), BF),
            pltpu.VMEM((keys, rows_all), F32),
            pltpu.VMEM((keys, rows_all), BF),
        ],
        compiler_params=pltpu.CompilerParams(vmem_limit_bytes=32 << 20),
        cost_estimate=pl.CostEstimate(
            flops=keys * rows_all * HEAD * 10,
            bytes_accessed=4 << 20,
            transcendentals=keys * rows_all,
        ),
    )(
        pltpu.with_memory_space_constraint(q, pltpu.HBM),
        pltpu.with_memory_space_constraint(t, pltpu.HBM),
        win,
        own,
        attn,
    )


def prepare_kernel(k_ref, v_ref, ks_ref, vs_ref, docs_ref, row_ref, first_ref):
    tokens = k_ref.shape[0]
    k = (k_ref[...].astype(F32) + ks_ref[...]).astype(BF)
    v = (v_ref[...].astype(F32) + vs_ref[...]).astype(BF)
    docs = (docs_ref[...] + 1).astype(F32)
    docs = jnp.broadcast_to(docs, (TAIL, docs.shape[1])).astype(BF)
    for h in range(k.shape[1] // HEAD):
        at = 2 * h * HEAD
        row_ref[0:tokens, at : at + HEAD] = k[:, h * HEAD : (h + 1) * HEAD]
        row_ref[0:tokens, at + HEAD : at + 2 * HEAD] = v[:, h * HEAD : (h + 1) * HEAD]
        row_ref[tokens:, at : at + tokens] = docs
        row_ref[tokens:, at + HEAD : at + HEAD + tokens] = docs
    first_ref[...] = row_ref[:, 0 : 2 * HEAD]


def prepare(k, v, ks, vs, docs):
    tokens, width = k.shape
    hbm = [pltpu.with_memory_space_constraint(x, pltpu.HBM) for x in (k, v, ks, vs, docs)]
    return pl.pallas_call(
        prepare_kernel,
        out_shape=[
            jax.ShapeDtypeStruct((tokens + TAIL, 2 * width), BF),
            jax.ShapeDtypeStruct((tokens + TAIL, 2 * HEAD), BF),
        ],
        compiler_params=pltpu.CompilerParams(vmem_limit_bytes=4 << 20),
        cost_estimate=pl.CostEstimate(flops=1 << 17, bytes_accessed=1 << 19, transcendentals=0),
    )(*hbm)


def spread_kernel(x_ref, four_ref, three_ref, two_ref, one_ref, row_ref, out_ref):
    rows = row_ref.shape[0]
    for i in range(out_ref.shape[0]):
        @pl.when(i > x_ref[0])
        def _():
            out_ref[i, 0:rows, :] = row_ref[...]

        @pl.when(i <= x_ref[0])
        def _():
            out_ref[i, 0:rows, :] = four_ref[...]

        out_ref[i, rows : 2 * rows, :] = one_ref[...]
        out_ref[i, 2 * rows : 3 * rows, :] = two_ref[...]
        out_ref[i, 3 * rows :, :] = three_ref[...]


def spread(where_x, row, one, two, three, four, head, n):
    rows, width = row.shape[0], 2 * HEAD
    at_head = pl.BlockSpec((rows, width), lambda g: (0, head))
    below = 0 if four.shape[0] == rows else 1
    return pl.pallas_call(
        spread_kernel,
        grid=(1,),
        in_specs=[
            pl.BlockSpec(memory_space=pltpu.SMEM),
            pl.BlockSpec((rows, width), lambda g: (below, 0)),
            pl.BlockSpec((rows, width), lambda g: (0, 0)),
            at_head,
            at_head,
            at_head,
        ],
        out_specs=pl.BlockSpec(memory_space=pltpu.VMEM),
        out_shape=jax.ShapeDtypeStruct((n, ROWS * rows, width), BF),
        compiler_params=pltpu.CompilerParams(vmem_limit_bytes=8 << 20),
        cost_estimate=pl.CostEstimate(flops=0, bytes_accessed=2 << 20, transcendentals=0),
    )(where_x, four, three, two, one, row)


def fold_kernel(x_ref, back_ref, gown_ref, sent_ref, kept_ref):
    tokens = gown_ref.shape[0]
    n = back_ref.shape[0]

    def part(i, b):
        return back_ref[i, b * tokens : (b + 1) * tokens, :].astype(F32)

    own = gown_ref[...]
    last = jnp.zeros_like(own)
    for i in range(n):
        later = i > x_ref[0]
        p = part(i, 0)
        own = own + jnp.where(later, p, 0.0)
        last = last + jnp.where(later, 0.0, p)
    kept_ref[0:tokens, :] = own
    for b in (1, 2):
        kept_ref[b * tokens : (b + 1) * tokens, :] = sum(part(i, b) for i in range(n))
    sent_ref[0:tokens, :] = sum(part(i, 3) for i in range(n)).astype(BF)
    sent_ref[tokens:, :] = last.astype(BF)


def fold(where_x, back, gown):
    tokens, width = gown.shape
    vmem = pl.BlockSpec(memory_space=pltpu.VMEM)
    return pl.pallas_call(
        fold_kernel,
        in_specs=[pl.BlockSpec(memory_space=pltpu.SMEM), vmem, vmem],
        out_specs=[vmem, vmem],
        out_shape=[
            jax.ShapeDtypeStruct((2 * tokens, width), BF),
            jax.ShapeDtypeStruct((3 * tokens, width), F32),
        ],
        compiler_params=pltpu.CompilerParams(vmem_limit_bytes=8 << 20),
        cost_estimate=pl.CostEstimate(flops=1 << 19, bytes_accessed=2 << 20, transcendentals=0),
    )(where_x, back, gown)


def gather_kernel(n_tp, first_ref, plane_ref, near_ref, out_ref):
    square = jnp.sum(plane_ref[:, 2, :])
    out_ref[...] = jnp.full(out_ref.shape, square, F32)
    near_ref[...] = jnp.sum(plane_ref[pl.ds(first_ref[0], n_tp)], 0)


def gather(first, plane, n, n_tp):
    vmem = pl.BlockSpec(memory_space=pltpu.VMEM)
    return pl.pallas_call(
        functools.partial(gather_kernel, n_tp),
        in_specs=[pl.BlockSpec(memory_space=pltpu.SMEM), vmem],
        out_specs=[vmem, vmem],
        out_shape=[
            jax.ShapeDtypeStruct(plane.shape[1:], F32),
            jax.ShapeDtypeStruct((n, 1, plane.shape[2]), F32),
        ],
        compiler_params=pltpu.CompilerParams(vmem_limit_bytes=4 << 20),
        cost_estimate=pl.CostEstimate(flops=1 << 14, bytes_accessed=1 << 16, transcendentals=0),
    )(first, plane)


def update_kernel(count, all_ref, near_ref, ks_ref, vs_ref, grad_ref, nk_ref, nv_ref):
    tokens = ks_ref.shape[0]
    overall = jnp.sum(all_ref[...], 0)
    a = step_size / jnp.sqrt(overall / count + 1e-05)
    near = near_ref[...]
    size_sq = jnp.maximum(near[0:1] + 2.0 * a * near[1:2] + a * a * near[2:3], 0.0)
    radius = radius_scale * math.sqrt(2 * KV_HEADS * HEAD)
    factor = jnp.minimum(1.0, radius / jnp.sqrt(size_sq + 1e-06))
    factor = jnp.broadcast_to(factor, (tokens, tokens)).T
    for h in range(ks_ref.shape[1] // HEAD):
        part = slice(h * HEAD, (h + 1) * HEAD)
        nk_ref[:, part] = (ks_ref[:, part] + a * grad_ref[:, 2 * h * HEAD : (2 * h + 1) * HEAD]) * factor
        nv_ref[:, part] = (vs_ref[:, part] + a * grad_ref[:, (2 * h + 1) * HEAD : (2 * h + 2) * HEAD]) * factor


def update(count, everything, near, ks, vs, grad):
    return pl.pallas_call(
        functools.partial(update_kernel, count),
        out_shape=[jax.ShapeDtypeStruct(ks.shape, F32)] * 2,
        compiler_params=pltpu.CompilerParams(vmem_limit_bytes=4 << 20),
        cost_estimate=pl.CostEstimate(flops=1 << 17, bytes_accessed=1 << 20, transcendentals=256),
    )(everything, near, ks, vs, grad)


def along_z(x, d):
    n = lax.axis_size("cz")
    return lax.ppermute(x, "cz", [(i - d, i) for i in range(n) if 0 <= i - d < n])


def swap_x(x):
    return lax.all_to_all(x, "cx", 0, 0)


def sum_among(x, axes):
    n = math.prod(lax.axis_size(a) for a in axes)
    return lax.all_to_all(jnp.broadcast_to(x[None], (n,) + x.shape), axes, 0, 0)


def per_device(query, key, value, key_shift, value_shift, doc_ids, target):
    tokens = query.shape[1]
    kv_local = key.shape[2] // HEAD
    where_x = lax.axis_index("cx")
    n_x = lax.axis_size("cx")
    at_x = where_x.astype(jnp.int32)[None]
    row, row_first = prepare(key[0], value[0], key_shift[0], value_shift[0], doc_ids)
    four, three = along_z(row_first, 4), along_z(row_first, 3)
    two, one = along_z(row, 2), along_z(row, 1)
    wins = []
    for h in range(kv_local):
        if h > 0:
            part = slice(2 * h * HEAD, 2 * (h + 1) * HEAD)
            three = four = along_z(jnp.concatenate([one[:, part], two[:, part]], 0), 2)
        wins.append(swap_x(spread(at_x, row, one, two, three, four, h, n_x)))
    attn = query[0]
    kept = []
    for h in range(kv_local):
        attn, gwin, gown = attention(query[0], target[0], wins[h], row, attn, h)
        sent, mine = fold(at_x, swap_x(gwin), gown)
        kept.append((along_z(sent, -2), mine))
    near = [
        jnp.concatenate(
            [
                (mine[(b + 1) * tokens : (b + 2) * tokens] + far[b * tokens : (b + 1) * tokens]).astype(BF)
                for far, mine in kept
            ],
            1,
        )
        for b in range(2)
    ]
    two, one = along_z(near[1], -2), along_z(near[0], -1)
    own = jnp.concatenate([mine[:tokens] for _, mine in kept], 1)
    grad = two.astype(F32) + one.astype(F32) + own
    grad_key = jnp.concatenate(
        [grad[:, 2 * h * HEAD : (2 * h + 1) * HEAD] for h in range(kv_local)], 1
    )
    grad_val = jnp.concatenate(
        [grad[:, (2 * h + 1) * HEAD : (2 * h + 2) * HEAD] for h in range(kv_local)], 1
    )
    ks, vs = key_shift[0], value_shift[0]
    sums = jnp.stack(
        [
            jnp.sum(ks * ks, -1) + jnp.sum(vs * vs, -1),
            jnp.sum(ks * grad_key, -1) + jnp.sum(vs * grad_val, -1),
            jnp.sum(grad_key * grad_key, -1) + jnp.sum(grad_val * grad_val, -1),
        ]
    )
    n_dp, n_tp = lax.axis_size("dp"), lax.axis_size("tp")
    first = ((lax.axis_index("dp") * n_x + where_x) * n_tp).astype(jnp.int32)[None]
    sums, first = lax.optimization_barrier((sums, first))
    plane = sum_among(sums, ("dp", "cx", "tp"))
    near, square = gather(first, plane, lax.axis_size("cz"), n_tp)
    everything = lax.all_to_all(square, "cz", 0, 0)
    count = n_dp * tokens * n_x * lax.axis_size("cz") * 2 * KV_HEADS * HEAD
    new_ks, new_vs = update(count, everything, near, ks, vs, grad)
    return attn[None], new_ks[None], new_vs[None]


def solution(mesh):
    sizes = mesh.devices.shape
    inner = Mesh(
        mesh.devices.reshape(sizes[0], sizes[1] // 4, 4, sizes[2]), ("dp", "cz", "cx", "tp")
    )
    whole = P("dp", ("cz", "cx"), "tp")
    in_specs = (whole,) * 5 + (P("dp", ("cz", "cx")), whole)
    return jax.shard_map(
        per_device, mesh=inner, in_specs=in_specs, out_specs=(whole,) * 3, check_vma=False
    )
```
